512 devices in a mesh: expert: 32 (over z_lo, y, core), tensor: 16 (over z_hi, x).
Axes of the slice: x: 4, y: 8, z: 8 (z_hi: 4, z_lo: 2; z = z_hi * 2 + z_lo), core: 2. Of those that a mesh axis runs over, the one named last changes fastest.
Arguments:
- tokens: bfloat16 [4096, 4096], P('expert', 'tensor'), may hold values from -6 to 6
- routes: int32 [4096, 2], P('expert'), may hold values from 0 to 31, all different within a row; in each aligned block of 128 rows (0 to 127, 128 to 255, ...) at most 16 rows name the same one
- route_gates: float32 [4096, 2], P('expert'), may hold values from 0.1 to 0.6
- gate_weight: bfloat16 [32, 4096, 2048], P('expert', None, 'tensor'), may hold values from -0.09375 to 0.09375
- up_weight: bfloat16 [32, 4096, 2048], P('expert', None, 'tensor'), may hold values from -0.09375 to 0.09375
- down_weight: bfloat16 [32, 2048, 4096], P('expert', 'tensor'), may hold values from -0.1875 to 0.1875
Outputs:
- combined: bfloat16 [4096, 4096], P('expert', 'tensor')
The draws below stay inside these ranges and needn't reach their ends.
Inputs may be any that keep to these rules, and one draw needn't show every extreme that they name: Within each aligned block of 128 tokens no expert is named by more than 16 routes, and the 2 experts of one token differ.
All inputs are finite; a program needn't handle non-finite values.
Results may differ from the reference program's by a relative error of at most 0.02.
Values may be sent and summed in bfloat16 or wider, within the bound.
A program may use at most 64 MiB of HBM per device.

```python
import math
import jax
import jax.numpy as jnp
import numpy as np
from jax import lax

D = 4096
FF = 2048
ROUTES = 2
TOK_G = 128
EXPERTS = 32
CAP = 16
TOKENS = 4096
N_EXPERT = 32
N_TENSOR = 16


def raised(drawn, key, source, target, shards_of, factor):
    owner, partner = [(jnp.arange(drawn.shape[axis_at]) // (drawn.shape[axis_at] // shards_of)).reshape([-1 if axis == axis_at else 1 for axis in range(drawn.ndim)]) for axis_at in (source, target)]
    chosen = jax.random.permutation(key, shards_of)[partner]
    strong = (owner == chosen) | (owner == (partner + shards_of // 2) % shards_of)
    return jnp.where(strong, factor * drawn, drawn)


def steps_of(own_key, extent, pieces, low, largest):
    gain, own = 1.0, jax.random.fold_in(own_key, 6)
    for position, blocks in pieces:
        draws = jnp.exp(jax.random.uniform(jax.random.fold_in(own, position), (blocks,), jnp.float32, low / len(pieces), largest / len(pieces)))
        gain = gain * jnp.repeat(draws, extent[position] // blocks).reshape([-1 if axis == position else 1 for axis in range(len(extent))])
    return gain


def assign_block(key, own, number, rows, number_of, top, bound, skew):
    order = jax.random.permutation(key, number_of)
    crowded, ordinary = load_shares(number_of, rows * top, bound, skew, True), load_shares(number_of, rows * top, bound, skew, False)
    places = jnp.arange(number_of)

    def named(tallies, rotation):
        used = int((tallies > 0).sum())
        fixed = max(1, used // 4)
        passed = fixed + (places - fixed + rotation * (used - fixed)) % max(1, number_of - fixed)
        return jnp.zeros((number_of,), jnp.int32).at[order[jnp.where(places < fixed, places, passed)]].set(jnp.asarray(tallies, jnp.int32))

    tallies = jnp.where(number % 4 == 0, named(crowded, number // 4), named(ordinary, number - number // 4 - 1))
    mixed = jax.random.permutation(jax.random.fold_in(own, 3), number_of)
    giver, receiver = mixed[0:number_of // 2 * 2:2], mixed[1:number_of // 2 * 2:2]
    slack = jnp.minimum(tallies[giver] - 1, bound - tallies[receiver]) // 2
    slack = jnp.where((giver == order[0]) | (receiver == order[0]) | (tallies[receiver] == 0), 0, jnp.maximum(slack, 0))
    passed = jax.random.randint(jax.random.fold_in(own, 4), (number_of // 2,), 0, 1 << 20) % (slack + 1)
    tallies = tallies.at[giver].add(-passed).at[receiver].add(passed)
    members = jnp.searchsorted(jnp.cumsum(tallies), jnp.arange(rows * top), side="right").astype(jnp.int32)
    listing = members.reshape(top, rows).T
    listing = listing[jax.random.permutation(jax.random.fold_in(own, 1), rows)]
    rotation = jax.random.randint(jax.random.fold_in(own, 2), (rows, 1), 0, top)
    return jnp.take_along_axis(listing, (jnp.arange(top)[None, :] + rotation) % top, axis=1)


def load_shares(amount, total, most, lean, full):
    weights = [(1 << 20) // math.isqrt(grade ** lean) + 1 for grade in range(1, amount + 1)]
    largest = most if full else min(most, max(-(-total // amount), total * weights[0] // sum(weights)))
    least = 1 if total - largest >= amount - 1 else 0
    given, spare = [largest] + [least] * (amount - 1), total - largest - least * (amount - 1)
    while spare > 0:
        movable = [i for i in range(1, amount) if given[i] < largest] or [i for i in range(1, amount) if given[i] < most]
        whole, budget = sum([weights[i] for i in movable]), spare
        for i in movable:
            more = min(most - given[i], max(1, budget * weights[i] // whole), spare)
            given[i] = given[i] + more
            spare = spare - more
    return np.array(given)


def bell_draw(key, extent, spread, most, pieces=(), held_as=jnp.bfloat16):
    values = jax.random.normal(key, extent, jnp.float32) * spread
    if len(pieces) > 0:
        values = steps_of(key, extent, pieces, -0.22, 0.18) * values
    return jnp.clip(values, min=-most, max=most).astype(held_as)


def gaussian_with(stream_key, extent, deviation, reach, pieces, heavy, kind=jnp.bfloat16):
    values = deviation * jax.random.normal(stream_key, extent, jnp.float32)
    if pieces:
        values = values * steps_of(stream_key, extent, pieces, -0.22, 0.18)
    return jnp.clip(raised(values, jax.random.fold_in(stream_key, 3), *heavy), -reach, reach).astype(kind)


def setup_inputs(seed: int = 0) -> dict:
    key_of = jax.random.split(jax.random.key(seed), 7)
    tokens = bell_draw(key_of[0], (TOKENS, D), 1.0, 6.0, ((0, 32), (1, 16)))
    routes_keys = jax.random.split(jax.random.fold_in(key_of[1], 1), TOKENS // TOK_G)
    routes_turns = jax.random.permutation(jax.random.fold_in(key_of[1], 3), TOKENS // TOK_G)
    routes = jax.vmap(lambda own, number: assign_block(jax.random.fold_in(key_of[1], 2), own, number, TOK_G, EXPERTS, ROUTES, CAP, 2))(routes_keys, routes_turns).reshape((TOKENS, ROUTES))
    route_gates = jnp.clip(0.1 + 0.5 * jax.random.uniform(key_of[2], (TOKENS, ROUTES), jnp.float32) ** steps_of(key_of[2], (TOKENS, ROUTES), ((0, 32),), -0.2, 0.2), 0.1, 0.6)
    gate_weight = bell_draw(key_of[3], (EXPERTS, D, FF), D ** -0.5, 0.09375, ((0, 32), (2, 16)))
    up_weight = bell_draw(key_of[4], (EXPERTS, D, FF), D ** -0.5, 0.09375, ((0, 32), (2, 16)))
    down_weight = gaussian_with(key_of[5], (EXPERTS, FF, D), FF ** -0.5, 0.1875, ((0, 32), (1, 16)), (1, 2, 16, 2.0))
    return {"tokens": tokens, "routes": routes, "route_gates": route_gates, "gate_weight": gate_weight, "up_weight": up_weight, "down_weight": down_weight}


def reference(tokens, routes, route_gates, gate_weight, up_weight, down_weight):
    slot_total = N_EXPERT * CAP
    grouped = routes.reshape(N_EXPERT, TOK_G * ROUTES)
    onehot = (grouped[:, :, None] == jnp.arange(EXPERTS, dtype=jnp.int32)[None, None, :]).astype(jnp.int32)
    before = jnp.cumsum(onehot, axis=1) - onehot
    slot_ids = jnp.sum(before * onehot, axis=2).reshape(TOKENS, ROUTES).astype(jnp.int32)
    source_ids = (jnp.arange(TOKENS, dtype=jnp.int32) // TOK_G)[:, None]
    places = (source_ids * CAP + slot_ids).astype(jnp.int32)
    repeated = jnp.repeat(tokens, ROUTES, axis=0)

    def one_expert(expert):
        target = jnp.where(routes == expert, places, slot_total).reshape(-1).astype(jnp.int32)
        received = jnp.zeros((slot_total, D), jnp.bfloat16).at[target].set(repeated, mode="drop")
        gate_proj = jnp.dot(received, gate_weight[expert], preferred_element_type=jnp.float32)
        up_proj = jnp.dot(received, up_weight[expert], preferred_element_type=jnp.float32)
        hidden = (jax.nn.silu(gate_proj) * up_proj).astype(jnp.bfloat16)
        hidden_blocks = hidden.reshape(slot_total, N_TENSOR, FF // N_TENSOR).transpose(1, 0, 2)
        down_blocks = down_weight[expert].reshape(N_TENSOR, FF // N_TENSOR, D)

        def add_block(totals, pair):
            partial_value = jnp.dot(pair[0], pair[1], preferred_element_type=jnp.float32).astype(jnp.bfloat16)
            partial_value = lax.optimization_barrier(partial_value)
            return totals + partial_value.astype(jnp.float32), None

        summed, unused = lax.scan(add_block, jnp.zeros((slot_total, D), jnp.float32), (hidden_blocks, down_blocks))
        return summed.astype(jnp.bfloat16)

    expert_out = lax.map(one_expert, jnp.arange(EXPERTS, dtype=jnp.int32))
    flat_out = expert_out.reshape(EXPERTS * slot_total, D)
    lookup = (routes * slot_total + places).reshape(-1).astype(jnp.int32)
    picked = flat_out[lookup].astype(jnp.float32).reshape(TOKENS, ROUTES, D)
    combined = jnp.sum(picked * route_gates[:, :, None], axis=1)
    return combined.astype(jnp.bfloat16)
```

```python
import jax
import jax.numpy as jnp
from jax import lax
from jax.experimental import pallas as pl
from jax.experimental.pallas import tpu as pltpu
from jax.sharding import PartitionSpec as P

MESH = pl.DeviceIdType.MESH
F32, BF16 = jnp.float32, jnp.bfloat16
CHUNKS = 4
RING = 4


def remote(src, dst, send, recv, device):
    return pltpu.make_async_remote_copy(
        src_ref=src, dst_ref=dst, send_sem=send, recv_sem=recv, device_id=device, device_id_type=MESH
    )


def layer(
    tok, routes, gates, gate_hbm, up_hbm, down_hbm, out,
    outgoing, xs, ps, x_one, x_two, z_one, z_two, back, w_in, w_out,
    w_sem, a_send, a_recv, gz_send, gz_recv, gx_send, gx_recv,
    sx_send, sx_recv, sz_send, sz_recv, b_send, b_recv,
):
    e, t = lax.axis_index("expert"), lax.axis_index("tensor")
    core, y, zl = e % 2, (e // 2) % 8, e // 16
    x, zh = t % RING, t // RING
    x_up, x_far, x_dn = (x + 1) % RING, (x + 2) % RING, (x + 3) % RING
    z_up, z_far, z_dn = (zh + 1) % RING, (zh + 2) % RING, (zh + 3) % RING
    to_xu, to_xd = (e, zh * RING + x_up), (e, zh * RING + x_dn)
    to_zu, to_zd = (e, z_up * RING + x), (e, z_dn * RING + x)
    experts, cap = 32, 16
    tokens, width = tok.shape
    rows = xs.shape[3]
    half = rows // 2
    per = rows // cap

    def partner(j, sign):
        k, f = j // 4, j % 4
        dy = (k % 2) * ((k + 1) // 2) - (1 - k % 2) * (k // 2)
        return (((zl + f // 2) % 2) * 8 + (y + sign * dy + 8) % 8) * 2 + (core + f % 2) % 2

    def slot(i):
        return pl.ds(pl.multiple_of(i * cap, cap), cap)

    barrier = pltpu.get_barrier_semaphore()

    def greet(j, carry):
        pl.semaphore_signal(barrier, inc=1, device_id=(partner(j, 1), t), device_id_type=MESH)
        return carry

    lax.fori_loop(1, experts, greet, 0)
    for device in (to_xu, to_xd, to_zu, to_zd):
        pl.semaphore_signal(barrier, inc=1, device_id=device, device_id_type=MESH)

    hidden_block = gate_hbm.shape[1]
    loads = [
        pltpu.make_async_copy(gate_hbm, w_in.at[:, pl.ds(0, hidden_block)], w_sem.at[0]),
        pltpu.make_async_copy(up_hbm, w_in.at[:, pl.ds(hidden_block, hidden_block)], w_sem.at[1]),
        pltpu.make_async_copy(down_hbm, w_out, w_sem.at[2]),
    ]
    for load in loads:
        load.start()

    first, second = routes[0:1, :], routes[1:2, :]
    names = lax.broadcasted_iota(jnp.int32, (experts, tokens), 0)
    one, two = names == first, names == second
    count = (jnp.where(one, 1.0, 0.0) + jnp.where(two, 1.0, 0.0)).astype(BF16)
    earlier = lax.broadcasted_iota(jnp.int32, (tokens, tokens), 0) < lax.broadcasted_iota(
        jnp.int32, (tokens, tokens), 1
    )
    before = jnp.dot(count, jnp.where(earlier, 1.0, 0.0).astype(BF16), preferred_element_type=F32)
    place_one = first.astype(F32) * cap + jnp.sum(jnp.where(one, before, 0.0), axis=0, keepdims=True)
    place_two = second.astype(F32) * cap + jnp.sum(jnp.where(two, before, 0.0), axis=0, keepdims=True)
    places = lax.broadcasted_iota(jnp.int32, (experts * cap, tokens), 0).astype(F32)
    at_one, at_two = places == place_one, places == place_two
    picks = (jnp.where(at_one, 1.0, 0.0) + jnp.where(at_two, 1.0, 0.0)).astype(BF16)
    outgoing[...] = jnp.dot(picks, tok[...], preferred_element_type=F32).astype(BF16)

    pl.semaphore_wait(barrier, experts - 1 + 4)

    def dispatch(j, carry):
        d = partner(j, -1)
        remote(
            outgoing.at[slot(d)], xs.at[x, j // per, zh, slot(j % per)], a_send, a_recv.at[j], (d, t)
        ).start()
        return carry

    lax.fori_loop(1, experts, dispatch, 0)
    xs[x, 0, zh, pl.ds(0, cap), :] = outgoing[slot(e), :]
    for load in loads:
        load.wait()

    def arrived(ref, sem):
        remote(ref, ref, gz_send, sem, to_zu).wait_recv()

    def gather_z(c):
        def wait(j, carry):
            @pl.when(j > 0)
            def _():
                arrived(outgoing.at[slot(0)], a_recv.at[j])

            return carry

        lax.fori_loop(c * per, c * per + per, wait, 0)
        own = xs.at[x, c, zh]
        remote(own, own, gz_send, gz_recv.at[0, c], to_zu).start()
        remote(own, own, gz_send, gz_recv.at[1, c], to_zd).start()

    def forward_z(c):
        arrived(xs.at[x, c, z_dn], gz_recv.at[0, c])
        low = xs.at[x, c, z_dn, pl.ds(0, half)]
        remote(low, low, gz_send, gz_recv.at[2, c], to_zu).start()
        arrived(xs.at[x, c, z_up], gz_recv.at[1, c])
        high = xs.at[x, c, z_up, pl.ds(half, half)]
        remote(high, high, gz_send, gz_recv.at[3, c], to_zd).start()

    def gather_x(c):
        arrived(xs.at[x, c, z_far, pl.ds(0, half)], gz_recv.at[2, c])
        arrived(xs.at[x, c, z_far, pl.ds(half, half)], gz_recv.at[3, c])
        own = xs.at[x, c]
        remote(own, own, gx_send, gx_recv.at[0, c], to_xu).start()
        remote(own, own, gx_send, gx_recv.at[1, c], to_xd).start()

    def forward_x(c):
        arrived(xs.at[x_dn, c], gx_recv.at[0, c])
        low = xs.at[x_dn, c, pl.ds(0, 2)]
        remote(low, low, gx_send, gx_recv.at[2, c], to_xu).start()
        arrived(xs.at[x_up, c], gx_recv.at[1, c])
        high = xs.at[x_up, c, pl.ds(2, 2)]
        remote(high, high, gx_send, gx_recv.at[3, c], to_xd).start()

    def feed_forward(c):
        arrived(xs.at[x_far, c, pl.ds(0, 2)], gx_recv.at[2, c])
        arrived(xs.at[x_far, c, pl.ds(2, 2)], gx_recv.at[3, c])
        total = jnp.zeros((rows, 2 * hidden_block), F32)
        for block in range(RING * RING):
            total += jnp.dot(
                xs[block % RING, c, block // RING],
                w_in[block * width : (block + 1) * width, :],
                preferred_element_type=F32,
            )
        gate, up = total[:, :hidden_block], total[:, hidden_block:]
        hidden = (gate / (1.0 + jnp.exp(-gate)) * up).astype(BF16)
        for block in range(RING * RING):
            ps[block % RING, c, block // RING] = jnp.dot(
                hidden, w_out[:, block * width : (block + 1) * width], preferred_element_type=F32
            ).astype(BF16)
        remote(ps.at[x_far, c, pl.ds(0, 2)], x_one.at[0, c], sx_send, sx_recv.at[0, c], to_xu).start()
        remote(ps.at[x_far, c, pl.ds(2, 2)], x_one.at[1, c], sx_send, sx_recv.at[1, c], to_xd).start()
        remote(
            ps.at[x_up, c, pl.ds(2, 2)], x_two.at[0, c, pl.ds(2, 2)], sx_send, sx_recv.at[2, c], to_xu
        ).start()
        remote(
            ps.at[x_dn, c, pl.ds(0, 2)], x_two.at[1, c, pl.ds(0, 2)], sx_send, sx_recv.at[3, c], to_xd
        ).start()

    def add(*terms):
        return sum(term.astype(F32) for term in terms).astype(BF16)

    def relay_x(c):
        arrived(x_one.at[0, c], sx_recv.at[0, c])
        ps[x_up, c, 0:2] = add(ps[x_up, c, 0:2], x_one[0, c])
        remote(
            ps.at[x_up, c, pl.ds(0, 2)], x_two.at[0, c, pl.ds(0, 2)], sx_send, sx_recv.at[4, c], to_xu
        ).start()
        arrived(x_one.at[1, c], sx_recv.at[1, c])
        ps[x_dn, c, 2:4] = add(ps[x_dn, c, 2:4], x_one[1, c])
        remote(
            ps.at[x_dn, c, pl.ds(2, 2)], x_two.at[1, c, pl.ds(2, 2)], sx_send, sx_recv.at[5, c], to_xd
        ).start()

    def scatter_z(c):
        arrived(x_two.at[0, c, pl.ds(2, 2)], sx_recv.at[2, c])
        arrived(x_two.at[1, c, pl.ds(0, 2)], sx_recv.at[3, c])
        arrived(x_two.at[0, c, pl.ds(0, 2)], sx_recv.at[4, c])
        arrived(x_two.at[1, c, pl.ds(2, 2)], sx_recv.at[5, c])
        ps[x, c] = add(ps[x, c], x_two[0, c], x_two[1, c])
        low, high = pl.ds(0, half), pl.ds(half, half)
        remote(ps.at[x, c, z_far, low], z_one.at[0, c], sz_send, sz_recv.at[0, c], to_zu).start()
        remote(ps.at[x, c, z_far, high], z_one.at[1, c], sz_send, sz_recv.at[1, c], to_zd).start()
        remote(ps.at[x, c, z_up, high], z_two.at[0, c, high], sz_send, sz_recv.at[2, c], to_zu).start()
        remote(ps.at[x, c, z_dn, low], z_two.at[1, c, low], sz_send, sz_recv.at[3, c], to_zd).start()

    def relay_z(c):
        low, high = pl.ds(0, half), pl.ds(half, half)
        arrived(z_one.at[0, c], sz_recv.at[0, c])
        ps[x, c, z_up, 0:half] = add(ps[x, c, z_up, 0:half], z_one[0, c])
        remote(ps.at[x, c, z_up, low], z_two.at[0, c, low], sz_send, sz_recv.at[4, c], to_zu).start()
        arrived(z_one.at[1, c], sz_recv.at[1, c])
        ps[x, c, z_dn, half:rows] = add(ps[x, c, z_dn, half:rows], z_one[1, c])
        remote(ps.at[x, c, z_dn, high], z_two.at[1, c, high], sz_send, sz_recv.at[5, c], to_zd).start()

    def give_back(c):
        low, high = pl.ds(0, half), pl.ds(half, half)
        arrived(z_two.at[0, c, high], sz_recv.at[2, c])
        arrived(z_two.at[1, c, low], sz_recv.at[3, c])
        arrived(z_two.at[0, c, low], sz_recv.at[4, c])
        arrived(z_two.at[1, c, high], sz_recv.at[5, c])
        ps[x, c, zh] = add(ps[x, c, zh], z_two[0, c], z_two[1, c])

        def send(i, carry):
            j = c * per + i

            @pl.when(j > 0)
            def _():
                remote(
                    ps.at[x, c, zh, slot(i)], back.at[slot(e)], b_send, b_recv.at[e], (partner(j, 1), t)
                ).start()

            return carry

        lax.fori_loop(0, per, send, 0)

    stages = (
        gather_z, forward_z, gather_x, forward_x, feed_forward, relay_x, scatter_z, relay_z, give_back
    )

    def tick(s, carry):
        for number, stage in enumerate(stages):
            c = s - number

            @pl.when((c >= 0) & (c < CHUNKS))
            def _(stage=stage, c=c):
                stage(c)

        return carry

    lax.fori_loop(0, CHUNKS + len(stages) - 1, tick, 0)

    back[slot(e), :] = ps[x, 0, zh, pl.ds(0, cap), :]

    def collect(j, carry):
        @pl.when(j != e)
        def _():
            arrived(back.at[slot(0)], b_recv.at[j])

        return carry

    lax.fori_loop(0, experts, collect, 0)
    share = jnp.where(at_one, gates[0:1, :], 0.0) + jnp.where(at_two, gates[1:2, :], 0.0)
    coarse = share.astype(BF16)
    fine = (share - coarse.astype(F32)).astype(BF16)
    contract = (((0,), (0,)), ((), ()))
    returned = back[...]
    combined = lax.dot_general(coarse, returned, contract, preferred_element_type=F32)
    combined += lax.dot_general(fine, returned, contract, preferred_element_type=F32)
    out[...] = combined.astype(BF16)

    def sent(ref, sem):
        remote(ref, ref, sem, sz_recv.at[0, 0], to_zu).wait_send()

    most = pl.ds(0, (experts - 1) * cap)
    sent(outgoing.at[most], a_send)
    sent(back.at[most], b_send)
    sent(xs.at[0, pl.ds(0, 3)] if CHUNKS == 4 else xs.at[0, :, pl.ds(0, 3)], gz_send)
    sent(xs.at[pl.ds(0, 3)], gx_send)
    sent(ps.at[pl.ds(0, 3)], sx_send)
    sent(ps.at[0, pl.ds(0, 3)] if CHUNKS == 4 else ps.at[0, :, pl.ds(0, 3)], sz_send)


def shards(tokens, routes, route_gates, gate_weight, up_weight, down_weight):
    token_count, width = tokens.shape
    depth, block = gate_weight.shape[1:]
    experts, cap = 32, 16
    rows = experts * cap // CHUNKS
    dma, vmem = pltpu.SemaphoreType.DMA, pltpu.VMEM
    whole, left = pl.BlockSpec(memory_space=vmem), pl.BlockSpec(memory_space=pl.ANY)
    return pl.pallas_call(
        layer,
        out_shape=jax.ShapeDtypeStruct((token_count, width), BF16),
        in_specs=[whole, whole, whole, left, left, left],
        out_specs=whole,
        scratch_shapes=[
            vmem((experts * cap, width), BF16),
            vmem((RING, CHUNKS, RING, rows, width), BF16),
            vmem((RING, CHUNKS, RING, rows, width), BF16),
            vmem((2, CHUNKS, 2, rows, width), BF16),
            vmem((2, CHUNKS, RING, rows, width), BF16),
            vmem((2, CHUNKS, rows // 2, width), BF16),
            vmem((2, CHUNKS, rows, width), BF16),
            vmem((experts * cap, width), BF16),
            vmem((depth, 2 * block), BF16),
            vmem((block, depth), BF16),
            dma((3,)),
            dma,
            dma((experts,)),
            dma,
            dma((4, CHUNKS)),
            dma,
            dma((4, CHUNKS)),
            dma,
            dma((6, CHUNKS)),
            dma,
            dma((6, CHUNKS)),
            dma,
            dma((experts,)),
        ],
        compiler_params=pltpu.CompilerParams(
            collective_id=0, has_side_effects=True, vmem_limit_bytes=40 * 1024 * 1024
        ),
    )(tokens, routes.T, route_gates.T, gate_weight[0], up_weight[0], down_weight[0])


def solution(mesh):
    return jax.shard_map(
        shards,
        mesh=mesh,
        in_specs=(
            P("expert", "tensor"),
            P("expert", None),
            P("expert", None),
            P("expert", None, "tensor"),
            P("expert", None, "tensor"),
            P("expert", "tensor", None),
        ),
        out_specs=P("expert", "tensor"),
        check_vma=False,
    )
```

```python
import jax
import jax.numpy as jnp
from jax import lax
from jax.experimental import pallas as pl
from jax.experimental.pallas import tpu as pltpu
from jax.sharding import PartitionSpec as P

MESH = pl.DeviceIdType.MESH
F32, BF16 = jnp.float32, jnp.bfloat16
RING = 4
EXPERTS, CAP, CHUNKS = 32, 16, 4
PER = EXPERTS // CHUNKS
ROWS = PER * CAP
HOME = EXPERTS - 4


def remote(src, dst, send, recv, device):
    return pltpu.make_async_remote_copy(
        src_ref=src, dst_ref=dst, send_sem=send, recv_sem=recv, device_id=device, device_id_type=MESH
    )


def arrived(ref, sem, device):
    remote(ref, ref, sem, sem, device).wait_recv()


def sent(ref, sem, device):
    remote(ref, ref, sem, sem, device).wait_send()


def layer(
    tok_hbm, routes_hbm, gates_hbm, gate_hbm, up_hbm, down_hbm, out,
    tz, routes, gates, outgoing, xs, w_in, w_in_relay, w_out, w_out_relay,
    gu_out, gu_own, gu_in, hs, ps, back, share, cz, zr,
    l_sem, t_send, t_recv, wi_send, wi_recv, wo_send, wo_recv, a_send, a_recv,
    g_send, g_recv, h_send, h_recv, b_send, b_recv, z_send, z_recv,
):
    e, t = lax.axis_index("expert"), lax.axis_index("tensor")
    core, y, zl = e % 2, (e // 2) % 8, e // 16
    x, zh = t % RING, t // RING
    x_up, x_dn = (x + 1) % RING, (x + 3) % RING
    xu, xd = (e, zh * RING + x_up), (e, zh * RING + x_dn)
    tokens, width = out.shape
    block = w_in.shape[-1]

    def over_x(k):
        return (e, zh * RING + (x + k) % RING)

    def over_z(k):
        return (e, ((zh + k) % RING) * RING + x)

    def partner(j, sign):
        k, f = 7 - j // 4, j % 4
        dy = (k % 2) * ((k + 1) // 2) - (1 - k % 2) * (k // 2)
        return (((zl + f // 2) % 2) * 8 + (y + sign * dy + 8) % 8) * 2 + (core + f % 2) % 2

    barrier = pltpu.get_barrier_semaphore()

    def greet(j, carry):
        @pl.when(j != HOME)
        def _():
            pl.semaphore_signal(barrier, inc=1, device_id=(partner(j, 1), t), device_id_type=MESH)

        return carry

    for k in (1, 2, 3):
        pl.semaphore_signal(barrier, inc=1, device_id=over_z(k), device_id_type=MESH)
        pl.semaphore_signal(barrier, inc=1, device_id=over_x(k), device_id_type=MESH)
    lax.fori_loop(0, EXPERTS, greet, 0)

    smalls = [
        pltpu.make_async_copy(tok_hbm, tz.at[zh], l_sem.at[0]),
        pltpu.make_async_copy(routes_hbm, routes, l_sem.at[1]),
        pltpu.make_async_copy(gates_hbm, gates, l_sem.at[2]),
    ]
    mine = pl.ds(pl.multiple_of(x * block, block), block)
    loads_in = [
        pltpu.make_async_copy(gate_hbm.at[:, x], w_in.at[0, x], l_sem.at[3]),
        pltpu.make_async_copy(up_hbm.at[:, x], w_in.at[1, x], l_sem.at[4]),
    ]

    def columns(b, n):
        return pl.ds(pl.multiple_of((b * RING + n) * width, width), width)

    loads_out = [
        pltpu.make_async_copy(down_hbm.at[:, columns(b, x)], w_out.at[b, mine], l_sem.at[5 + b])
        for b in range(RING)
    ]
    for load in smalls:
        load.start()
    for load in smalls:
        load.wait()
    pl.semaphore_wait(barrier, EXPERTS - 1 + 6)

    for k in (2, 1, 3):
        remote(tz.at[zh], tz.at[zh], t_send, t_recv.at[k], over_z(k)).start()
    x_far = (x + 2) % RING
    remote(gate_hbm.at[:, x_far], w_in_relay.at[0], wi_send, wi_recv.at[0], xu).start()
    remote(up_hbm.at[:, x_far], w_in_relay.at[1], wi_send, wi_recv.at[1], xd).start()
    remote(gate_hbm.at[:, x_up], w_in.at[0, x], wi_send, wi_recv.at[2], xu).start()
    remote(gate_hbm.at[:, x_dn], w_in.at[0, x], wi_send, wi_recv.at[3], xd).start()
    remote(up_hbm.at[:, x_up], w_in.at[1, x], wi_send, wi_recv.at[4], xu).start()
    remote(up_hbm.at[:, x_dn], w_in.at[1, x], wi_send, wi_recv.at[5], xd).start()
    for load in loads_in + loads_out:
        load.start()

    first, second = routes[0:1, :], routes[1:2, :]
    names = lax.broadcasted_iota(jnp.int32, (EXPERTS, tokens), 0)
    one, two = names == first, names == second
    count = (jnp.where(one, 1.0, 0.0) + jnp.where(two, 1.0, 0.0)).astype(BF16)
    earlier = lax.broadcasted_iota(jnp.int32, (tokens, tokens), 0) < lax.broadcasted_iota(
        jnp.int32, (tokens, tokens), 1
    )
    before = jnp.dot(count, jnp.where(earlier, 1.0, 0.0).astype(BF16), preferred_element_type=F32)
    place_one = first.astype(F32) * CAP + jnp.sum(jnp.where(one, before, 0.0), axis=0, keepdims=True)
    place_two = second.astype(F32) * CAP + jnp.sum(jnp.where(two, before, 0.0), axis=0, keepdims=True)
    places = lax.broadcasted_iota(jnp.int32, (EXPERTS * CAP, tokens), 0).astype(F32)
    at_one, at_two = places == place_one, places == place_two
    picks = (jnp.where(at_one, 1.0, 0.0) + jnp.where(at_two, 1.0, 0.0)).astype(BF16)

    for k in (0, 1, 3, 2):
        n = (zh + 4 - k) % RING
        if k:
            arrived(tz.at[n], t_recv.at[k], over_z(1))
        picked = jnp.dot(picks, tz[n], preferred_element_type=F32).astype(BF16)
        outgoing[:, n] = picked.reshape(EXPERTS, CAP, width)

    def dispatch(j, carry):
        @pl.when(j != HOME)
        def _():
            d = partner(j, -1)
            remote(outgoing.at[d], xs.at[j // PER, j % PER], a_send, a_recv.at[j], (d, t)).start()

        return carry

    lax.fori_loop(0, EXPERTS, dispatch, 0)
    xs[HOME // PER, HOME % PER] = outgoing[e]

    arrived(w_in_relay.at[0], wi_recv.at[0], xu)
    remote(w_in_relay.at[0], w_in.at[0, x_dn], wi_send, wi_recv.at[6], xu).start()
    arrived(w_in_relay.at[1], wi_recv.at[1], xu)
    remote(w_in_relay.at[1], w_in.at[1, x_up], wi_send, wi_recv.at[7], xd).start()
    for b in (0, 1):
        remote(down_hbm.at[:, columns(b, x_far)], w_out_relay.at[0, b], wo_send, wo_recv.at[0], xu).start()
        remote(
            down_hbm.at[:, columns(b + 2, x_far)], w_out_relay.at[1, b], wo_send, wo_recv.at[1], xd
        ).start()
    for b in range(RING):
        remote(down_hbm.at[:, columns(b, x_up)], w_out.at[b, mine], wo_send, wo_recv.at[2], xu).start()
        remote(down_hbm.at[:, columns(b, x_dn)], w_out.at[b, mine], wo_send, wo_recv.at[3], xd).start()

    shared = jnp.where(at_one, gates[0:1, :], 0.0) + jnp.where(at_two, gates[1:2, :], 0.0)
    shared = shared.T
    coarse = shared.astype(BF16)
    share[0:tokens, :] = coarse
    share[tokens : 2 * tokens, :] = (shared - coarse.astype(F32)).astype(BF16)

    from_dn = pl.ds(pl.multiple_of(x_dn * block, block), block)
    from_up = pl.ds(pl.multiple_of(x_up * block, block), block)
    from_far = pl.ds(pl.multiple_of(x_far * block, block), block)

    for load in loads_in:
        load.wait()
    arrived(w_in.at[0, x_dn], wi_recv.at[2], xu)
    arrived(w_in.at[0, x_up], wi_recv.at[3], xu)
    arrived(w_in.at[1, x_dn], wi_recv.at[4], xu)
    arrived(w_in.at[1, x_up], wi_recv.at[5], xu)
    arrived(w_in.at[0, x_far], wi_recv.at[6], xu)
    arrived(w_in.at[1, x_far], wi_recv.at[7], xu)

    def project(c):
        def wait(i, carry):
            j = c * PER + i

            @pl.when(j != HOME)
            def _():
                arrived(xs.at[0, 0], a_recv.at[j], xu)

            return carry

        lax.fori_loop(0, PER, wait, 0)
        for k in (2, 1, 3, 0):
            n = (x + k) % RING
            total = jnp.zeros((ROWS, 2 * block), F32)
            for b in range(RING):
                weights = jnp.concatenate([w_in[0, n, b], w_in[1, n, b]], axis=1)
                total += jnp.dot(xs[c, :, b].reshape(ROWS, width), weights, preferred_element_type=F32)
            if k:
                gu_out[n, c] = total.astype(BF16)
                remote(gu_out.at[n, c], gu_in.at[k - 1, c], g_send, g_recv.at[k - 1, c], over_x(k)).start()
            else:
                gu_own[c] = total

    def activate(c):
        total = gu_own[c]
        for k in (1, 3, 2):
            arrived(gu_in.at[k - 1, c], g_recv.at[k - 1, c], xu)
            total += gu_in[k - 1, c].astype(F32)
        gate, up = total[:, :block], total[:, block:]
        hs[x, c] = (gate / (1.0 + jnp.exp(-gate)) * up).astype(BF16)
        for k in (2, 1, 3):
            remote(hs.at[x, c], hs.at[x, c], h_send, h_recv.at[k - 1, c], over_x(k)).start()

    def hand_on():
        arrived(w_out_relay.at[0], wo_recv.at[0], xu)
        low, high = pl.ds(0, 2), pl.ds(2, 2)
        remote(w_out_relay.at[0], w_out.at[low, from_dn], wo_send, wo_recv.at[4], xu).start()
        arrived(w_out_relay.at[1], wo_recv.at[1], xu)
        remote(w_out_relay.at[1], w_out.at[high, from_up], wo_send, wo_recv.at[5], xd).start()

    def have_out():
        for load in loads_out:
            load.wait()
        low, high = pl.ds(0, 2), pl.ds(2, 2)
        arrived(w_out.at[:, from_dn], wo_recv.at[2], xu)
        arrived(w_out.at[:, from_up], wo_recv.at[3], xu)
        arrived(w_out.at[low, from_far], wo_recv.at[4], xu)
        arrived(w_out.at[high, from_far], wo_recv.at[5], xu)

    def expand(c):
        for k in (1, 3, 2):
            n = (x + 4 - k) % RING
            arrived(hs.at[n, c], h_recv.at[k - 1, c], xu)
        hidden = jnp.concatenate([hs[n, c] for n in range(RING)], axis=1)
        for b in range(RING):
            part = jnp.dot(hidden, w_out[b], preferred_element_type=F32).astype(BF16)
            ps[c, :, b] = part.reshape(PER, CAP, width)

        def send(i, carry):
            j = c * PER + i

            @pl.when(j != HOME)
            def _():
                remote(ps.at[c, i], back.at[e], b_send, b_recv.at[e], (partner(j, 1), t)).start()

            return carry

        lax.fori_loop(0, PER, send, 0)

    def tick(s, carry):
        @pl.when(s < CHUNKS)
        def _():
            project(s)

        pl.when(s == 1)(hand_on)

        @pl.when((s >= 1) & (s <= CHUNKS))
        def _():
            activate(s - 1)

        pl.when(s == 2)(have_out)

        @pl.when(s >= 2)
        def _():
            expand(s - 2)

        return carry

    lax.fori_loop(0, CHUNKS + 2, tick, 0)
    back[e] = ps[HOME // PER, HOME % PER]

    def collect(j, carry):
        @pl.when(j != e)
        def _():
            arrived(back.at[0], b_recv.at[j], xu)

        return carry

    lax.fori_loop(0, EXPERTS, collect, 0)

    def combine(n):
        returned = back[:, n].reshape(EXPERTS * CAP, width)
        both = jnp.dot(share[...], returned, preferred_element_type=F32)
        return both[:tokens] + both[tokens:]

    for k in (2, 1, 3):
        n = (zh + k) % RING
        cz[n] = combine(n).astype(BF16)
        remote(cz.at[n], zr.at[k - 1], z_send, z_recv.at[k - 1], over_z(k)).start()
    total = combine(zh)
    for k in (1, 3, 2):
        arrived(zr.at[k - 1], z_recv.at[k - 1], xu)
        total += zr[k - 1].astype(F32)
    out[...] = total.astype(BF16)

    sent(tz.at[pl.ds(0, 3)], t_send, xu)
    sent(w_in, wi_send, xu)
    sent(w_out, wo_send, xu)
    sent(outgoing.at[pl.ds(0, EXPERTS - 1)], a_send, xu)
    sent(gu_out.at[pl.ds(0, 3)], g_send, xu)
    sent(hs.at[pl.ds(0, 3)], h_send, xu)
    sent(back.at[pl.ds(0, EXPERTS - 1)], b_send, xu)
    sent(cz.at[pl.ds(0, 3)], z_send, xu)


def shards(tokens, routes, route_gates, gate_weight, up_weight, down_weight):
    token_count, width = tokens.shape
    depth, block = gate_weight.shape[1:]
    dma, vmem = pltpu.SemaphoreType.DMA, pltpu.VMEM
    halves = (RING, RING, width, block)
    return pl.pallas_call(
        layer,
        out_shape=jax.ShapeDtypeStruct((token_count, width), BF16),
        in_specs=[pl.BlockSpec(memory_space=pltpu.HBM)] * 6,
        out_specs=pl.BlockSpec(memory_space=vmem),
        scratch_shapes=[
            vmem((RING, token_count, width), BF16),
            vmem((2, token_count), jnp.int32),
            vmem((2, token_count), F32),
            vmem((EXPERTS, RING, CAP, width), BF16),
            vmem((CHUNKS, PER, RING, CAP, width), BF16),
            vmem((2,) + halves, BF16),
            vmem((2,) + halves[1:], BF16),
            vmem((RING, RING * block, width), BF16),
            vmem((2, 2, block, width), BF16),
            vmem((RING, CHUNKS, ROWS, 2 * block), BF16),
            vmem((CHUNKS, ROWS, 2 * block), F32),
            vmem((RING - 1, CHUNKS, ROWS, 2 * block), BF16),
            vmem((RING, CHUNKS, ROWS, block), BF16),
            vmem((CHUNKS, PER, RING, CAP, width), BF16),
            vmem((EXPERTS, RING, CAP, width), BF16),
            vmem((2 * token_count, EXPERTS * CAP), BF16),
            vmem((RING, token_count, width), BF16),
            vmem((RING - 1, token_count, width), BF16),
            dma((5 + RING,)),
            dma,
            dma((RING,)),
            dma,
            dma((8,)),
            dma,
            dma((6,)),
            dma,
            dma((EXPERTS,)),
            dma,
            dma((RING - 1, CHUNKS)),
            dma,
            dma((RING - 1, CHUNKS)),
            dma,
            dma((EXPERTS,)),
            dma,
            dma((RING - 1,)),
        ],
        compiler_params=pltpu.CompilerParams(
            collective_id=0, has_side_effects=True, vmem_limit_bytes=62 * 1024 * 1024
        ),
    )(
        tokens,
        routes.T,
        route_gates.T,
        gate_weight.reshape(halves),
        up_weight.reshape(halves),
        down_weight[0],
    )


def solution(mesh):
    return jax.shard_map(
        shards,
        mesh=mesh,
        in_specs=(
            P("expert", "tensor"),
            P("expert", None),
            P("expert", None),
            P("expert", None, "tensor"),
            P("expert", None, "tensor"),
            P("expert", "tensor", None),
        ),
        out_specs=P("expert", "tensor"),
        check_vma=False,
    )
```

```python
import jax
import jax.numpy as jnp
from jax import lax
from jax.experimental import pallas as pl
from jax.experimental.pallas import tpu as pltpu
from jax.sharding import PartitionSpec as P

MESH = pl.DeviceIdType.MESH
F32, BF16 = jnp.float32, jnp.bfloat16
RING = 4
EXPERTS, CAP, CHUNKS = 32, 16, 4
PER = EXPERTS // CHUNKS
ROWS = PER * CAP
HOME = EXPERTS - 4
FAR = EXPERTS // 2
FAR_CHUNKS = CHUNKS // 2


def remote(src, dst, send, recv, device):
    return pltpu.make_async_remote_copy(
        src_ref=src, dst_ref=dst, send_sem=send, recv_sem=recv, device_id=device, device_id_type=MESH
    )


def arrived(ref, sem, device):
    remote(ref, ref, sem, sem, device).wait_recv()


def sent(ref, sem, device):
    remote(ref, ref, sem, sem, device).wait_send()


def layer(
    tok_hbm, routes_hbm, gates_hbm, gate_hbm, up_hbm, down_hbm, out,
    tz, routes, gates, out_far, out_near, xs, w_in, w_in_relay, w_out, w_out_relay,
    gu_out, gu_own, gu_in, hs, ps, zs, sums, back_far, back_near, share, cz, zr,
    l_sem, t_send, t_recv, wi_send, wi_recv, wo_send, wo_recv, f_send, a_send, a_recv, q_send, q_recv,
    g_send, g_recv, h_send, h_recv, r_send, r_recv, s_send, b_send, b_recv, z_send, z_recv,
):
    e, t = lax.axis_index("expert"), lax.axis_index("tensor")
    core, y, zl = e % 2, (e // 2) % 8, e // 16
    x, zh = t % RING, t // RING
    x_up, x_dn = (x + 1) % RING, (x + 3) % RING
    xu, xd = (e, zh * RING + x_up), (e, zh * RING + x_dn)
    tokens, width = out.shape
    block = w_in.shape[-1]

    def over_x(k):
        return (e, zh * RING + (x + k) % RING)

    def over_z(k):
        return (e, ((zh + k) % RING) * RING + x)

    def partner(j, sign):
        k, f = 7 - j // 4, j % 4
        dy = (k % 2) * ((k + 1) // 2) - (1 - k % 2) * (k // 2)
        return (((zl + f // 2) % 2) * 8 + (y + sign * dy + 8) % 8) * 2 + (core + f % 2) % 2

    barrier = pltpu.get_barrier_semaphore()

    def greet(j, carry):
        @pl.when(j != HOME)
        def _():
            pl.semaphore_signal(barrier, inc=1, device_id=(partner(j, 1), t), device_id_type=MESH)

        return carry

    for k in (1, 2, 3):
        pl.semaphore_signal(barrier, inc=1, device_id=over_z(k), device_id_type=MESH)
        pl.semaphore_signal(barrier, inc=1, device_id=over_x(k), device_id_type=MESH)
    lax.fori_loop(0, EXPERTS, greet, 0)

    smalls = [
        pltpu.make_async_copy(tok_hbm, tz.at[zh], l_sem.at[0]),
        pltpu.make_async_copy(routes_hbm, routes, l_sem.at[1]),
        pltpu.make_async_copy(gates_hbm, gates, l_sem.at[2]),
    ]
    mine = pl.ds(pl.multiple_of(x * block, block), block)
    loads_in = [
        pltpu.make_async_copy(gate_hbm.at[:, x], w_in.at[0, x], l_sem.at[3]),
        pltpu.make_async_copy(up_hbm.at[:, x], w_in.at[1, x], l_sem.at[4]),
    ]

    def columns(b, n):
        return pl.ds(pl.multiple_of((b * RING + n) * width, width), width)

    loads_out = [
        pltpu.make_async_copy(down_hbm.at[:, columns(b, x)], w_out.at[b, mine], l_sem.at[5 + b])
        for b in range(RING)
    ]
    for load in smalls:
        load.start()
    for load in smalls:
        load.wait()
    pl.semaphore_wait(barrier, EXPERTS - 1 + 6)

    for k in (2, 1, 3):
        remote(tz.at[zh], tz.at[zh], t_send, t_recv.at[k], over_z(k)).start()
    x_far = (x + 2) % RING
    remote(gate_hbm.at[:, x_far], w_in_relay.at[0], wi_send, wi_recv.at[0], xu).start()
    remote(up_hbm.at[:, x_far], w_in_relay.at[1], wi_send, wi_recv.at[1], xd).start()
    remote(gate_hbm.at[:, x_up], w_in.at[0, x], wi_send, wi_recv.at[2], xu).start()
    remote(gate_hbm.at[:, x_dn], w_in.at[0, x], wi_send, wi_recv.at[3], xd).start()

    first, second = routes[0:1, :], routes[1:2, :]
    names = lax.broadcasted_iota(jnp.int32, (EXPERTS, tokens), 0)
    one, two = names == first, names == second
    count = (jnp.where(one, 1.0, 0.0) + jnp.where(two, 1.0, 0.0)).astype(BF16)
    earlier = lax.broadcasted_iota(jnp.int32, (tokens, tokens), 0) < lax.broadcasted_iota(
        jnp.int32, (tokens, tokens), 1
    )
    before = jnp.dot(count, jnp.where(earlier, 1.0, 0.0).astype(BF16), preferred_element_type=F32)

    def listed(route):
        f = (((route >> 4) + zl) & 1) * 2 + ((route + core) & 1)
        m = (y - ((route >> 1) & 7)) & 7
        k = jnp.where(m <= 4, jnp.maximum(2 * m - 1, 0), 16 - 2 * m)
        return ((7 - k) * 4 + f).astype(F32)

    place_one = listed(first) * CAP + jnp.sum(jnp.where(one, before, 0.0), axis=0, keepdims=True)
    place_two = listed(second) * CAP + jnp.sum(jnp.where(two, before, 0.0), axis=0, keepdims=True)
    places = lax.broadcasted_iota(jnp.int32, (EXPERTS * CAP, tokens), 0).astype(F32)
    at_one, at_two = places == place_one, places == place_two
    picks = (jnp.where(at_one, 1.0, 0.0) + jnp.where(at_two, 1.0, 0.0)).astype(BF16)

    picked = jnp.dot(picks[: FAR * CAP], tz[zh], preferred_element_type=F32).astype(BF16)
    out_far[...] = picked.reshape(FAR, CAP, width)

    def dispatch_far(j, carry):
        remote(
            out_far.at[j], xs.at[j // PER, j % PER, zh], f_send, a_recv.at[j], (partner(j, -1), t)
        ).start()
        return carry

    lax.fori_loop(0, FAR, dispatch_far, 0)
    for k in (0, 1, 3, 2):
        n = (zh + 4 - k) % RING
        if k:
            arrived(tz.at[n], t_recv.at[k], xu)
        picked = jnp.dot(picks[FAR * CAP :], tz[n], preferred_element_type=F32).astype(BF16)
        out_near[:, n] = picked.reshape(EXPERTS - FAR, CAP, width)

    def dispatch_near(j, carry):
        @pl.when(j != HOME)
        def _():
            remote(
                out_near.at[j - FAR], xs.at[j // PER, j % PER], a_send, a_recv.at[j], (partner(j, -1), t)
            ).start()

        return carry

    lax.fori_loop(FAR, EXPERTS, dispatch_near, 0)
    xs[HOME // PER, HOME % PER] = out_near[HOME - FAR]
    for load in loads_in + loads_out:
        load.start()

    def spread(c, carry):
        def wait(i, inner):
            arrived(xs.at[0, 0, 0], a_recv.at[c * PER + i], xu)
            return inner

        lax.fori_loop(0, PER, wait, 0)
        for k in (2, 1, 3):
            own = xs.at[c, :, zh]
            remote(own, own, q_send, q_recv.at[k - 1, c], over_z(k)).start()
        return carry

    lax.fori_loop(0, FAR_CHUNKS, spread, 0)

    arrived(w_in_relay.at[0], wi_recv.at[0], xu)
    remote(w_in_relay.at[0], w_in.at[0, x_dn], wi_send, wi_recv.at[6], xu).start()
    arrived(w_in_relay.at[1], wi_recv.at[1], xu)
    remote(w_in_relay.at[1], w_in.at[1, x_up], wi_send, wi_recv.at[7], xd).start()
    remote(up_hbm.at[:, x_up], w_in.at[1, x], wi_send, wi_recv.at[4], xu).start()
    remote(up_hbm.at[:, x_dn], w_in.at[1, x], wi_send, wi_recv.at[5], xd).start()
    for b in (0, 1):
        remote(down_hbm.at[:, columns(b, x_far)], w_out_relay.at[0, b], wo_send, wo_recv.at[0], xu).start()
        remote(
            down_hbm.at[:, columns(b + 2, x_far)], w_out_relay.at[1, b], wo_send, wo_recv.at[1], xd
        ).start()
    for b in range(RING):
        remote(down_hbm.at[:, columns(b, x_up)], w_out.at[b, mine], wo_send, wo_recv.at[2], xu).start()
        remote(down_hbm.at[:, columns(b, x_dn)], w_out.at[b, mine], wo_send, wo_recv.at[3], xd).start()

    shared = jnp.where(at_one, gates[0:1, :], 0.0) + jnp.where(at_two, gates[1:2, :], 0.0)
    shared = shared.T
    coarse = shared.astype(BF16)
    share[0:tokens, :] = coarse
    share[tokens : 2 * tokens, :] = (shared - coarse.astype(F32)).astype(BF16)

    from_dn = pl.ds(pl.multiple_of(x_dn * block, block), block)
    from_up = pl.ds(pl.multiple_of(x_up * block, block), block)
    from_far = pl.ds(pl.multiple_of(x_far * block, block), block)

    for load in loads_in:
        load.wait()
    arrived(w_in.at[0, x_dn], wi_recv.at[2], xu)
    arrived(w_in.at[0, x_up], wi_recv.at[3], xu)
    arrived(w_in.at[1, x_dn], wi_recv.at[4], xu)
    arrived(w_in.at[1, x_up], wi_recv.at[5], xu)
    arrived(w_in.at[0, x_far], wi_recv.at[6], xu)
    arrived(w_in.at[1, x_far], wi_recv.at[7], xu)

    def project(c):
        @pl.when(c < FAR_CHUNKS)
        def _():
            for k in (1, 3, 2):
                arrived(xs.at[c, :, (zh + 4 - k) % RING], q_recv.at[k - 1, c], xu)

        @pl.when(c >= FAR_CHUNKS)
        def _():
            def wait(i, carry):
                j = c * PER + i

                @pl.when(j != HOME)
                def _():
                    arrived(xs.at[0, 0], a_recv.at[j], xu)

                return carry

            lax.fori_loop(0, PER, wait, 0)

        for k in (2, 1, 3, 0):
            n = (x + k) % RING
            total = jnp.zeros((ROWS, 2 * block), F32)
            for b in range(RING):
                weights = jnp.concatenate([w_in[0, n, b], w_in[1, n, b]], axis=1)
                total += jnp.dot(xs[c, :, b].reshape(ROWS, width), weights, preferred_element_type=F32)
            if k:
                gu_out[n, c] = total.astype(BF16)
                remote(gu_out.at[n, c], gu_in.at[k - 1, c], g_send, g_recv.at[k - 1, c], over_x(k)).start()
            else:
                gu_own[c] = total

    def activate(c):
        total = gu_own[c]
        for k in (1, 3, 2):
            arrived(gu_in.at[k - 1, c], g_recv.at[k - 1, c], xu)
            total += gu_in[k - 1, c].astype(F32)
        gate, up = total[:, :block], total[:, block:]
        hs[x, c] = (gate / (1.0 + jnp.exp(-gate)) * up).astype(BF16)
        for k in (2, 1, 3):
            remote(hs.at[x, c], hs.at[x, c], h_send, h_recv.at[k - 1, c], over_x(k)).start()

    def hand_on():
        arrived(w_out_relay.at[0], wo_recv.at[0], xu)
        low, high = pl.ds(0, 2), pl.ds(2, 2)
        remote(w_out_relay.at[0], w_out.at[low, from_dn], wo_send, wo_recv.at[4], xu).start()
        arrived(w_out_relay.at[1], wo_recv.at[1], xu)
        remote(w_out_relay.at[1], w_out.at[high, from_up], wo_send, wo_recv.at[5], xd).start()

    def have_out():
        for load in loads_out:
            load.wait()
        low, high = pl.ds(0, 2), pl.ds(2, 2)
        arrived(w_out.at[:, from_dn], wo_recv.at[2], xu)
        arrived(w_out.at[:, from_up], wo_recv.at[3], xu)
        arrived(w_out.at[low, from_far], wo_recv.at[4], xu)
        arrived(w_out.at[high, from_far], wo_recv.at[5], xu)

    def expand(c):
        for k in (1, 3, 2):
            n = (x + 4 - k) % RING
            arrived(hs.at[n, c], h_recv.at[k - 1, c], xu)
        hidden = jnp.concatenate([hs[n, c] for n in range(RING)], axis=1)
        for b in range(RING):
            part = jnp.dot(hidden, w_out[b], preferred_element_type=F32).astype(BF16)
            ps[c, :, b] = part.reshape(PER, CAP, width)

        @pl.when(c < FAR_CHUNKS)
        def _():
            for k in (2, 1, 3):
                remote(
                    ps.at[c, :, (zh + k) % RING], zs.at[k - 1, c], r_send, r_recv.at[k - 1, c], over_z(k)
                ).start()

        @pl.when(c >= FAR_CHUNKS)
        def _():
            def send(i, carry):
                j = c * PER + i

                @pl.when(j != HOME)
                def _():
                    remote(
                        ps.at[c, i], back_near.at[j - FAR], b_send, b_recv.at[j], (partner(j, 1), t)
                    ).start()

                return carry

            lax.fori_loop(0, PER, send, 0)

    def settle(c):
        total = ps[c, :, zh].astype(F32)
        for k in (1, 3, 2):
            arrived(zs.at[k - 1, c], r_recv.at[k - 1, c], xu)
            total += zs[k - 1, c].astype(F32)
        sums[c] = total.astype(BF16)

        def send(i, carry):
            j = c * PER + i
            remote(sums.at[c, i], back_far.at[j], s_send, b_recv.at[j], (partner(j, 1), t)).start()
            return carry

        lax.fori_loop(0, PER, send, 0)

    def tick(s, carry):
        @pl.when(s < CHUNKS)
        def _():
            project(s)

        pl.when(s == 1)(hand_on)

        @pl.when((s >= 1) & (s <= CHUNKS))
        def _():
            activate(s - 1)

        pl.when(s == 2)(have_out)

        @pl.when(s >= 2)
        def _():
            expand(s - 2)

        @pl.when((s >= 3) & (s < 3 + FAR_CHUNKS))
        def _():
            settle(s - 3)

        return carry

    lax.fori_loop(0, CHUNKS + 2, tick, 0)
    back_near[HOME - FAR] = ps[HOME // PER, HOME % PER]

    def collect_far(j, carry):
        arrived(back_far.at[0], b_recv.at[j], xu)
        return carry

    def collect_near(j, carry):
        @pl.when(j != HOME)
        def _():
            arrived(back_near.at[0], b_recv.at[j], xu)

        return carry

    def weigh(shares, returned):
        both = jnp.dot(shares, returned.reshape(FAR * CAP, width), preferred_element_type=F32)
        return both[:tokens] + both[tokens:]

    def combine(n):
        return weigh(share[:, FAR * CAP :], back_near[:, n])

    lax.fori_loop(0, FAR, collect_far, 0)
    total = weigh(share[:, : FAR * CAP], back_far[...])
    lax.fori_loop(FAR, EXPERTS, collect_near, 0)
    for k in (2, 1, 3):
        n = (zh + k) % RING
        cz[n] = combine(n).astype(BF16)
        remote(cz.at[n], zr.at[k - 1], z_send, z_recv.at[k - 1], over_z(k)).start()
    total += combine(zh)
    for k in (1, 3, 2):
        arrived(zr.at[k - 1], z_recv.at[k - 1], xu)
        total += zr[k - 1].astype(F32)
    out[...] = total.astype(BF16)

    sent(tz.at[pl.ds(0, 3)], t_send, xu)
    sent(w_in, wi_send, xu)
    sent(w_out, wo_send, xu)
    sent(out_far, f_send, xu)
    sent(out_near.at[pl.ds(0, EXPERTS - FAR - 1)], a_send, xu)
    some = (pl.ds(0, FAR_CHUNKS), slice(None), pl.ds(0, 3))
    sent(xs.at[some], q_send, xu)
    sent(ps.at[some], r_send, xu)
    sent(back_far, s_send, xu)
    sent(gu_out.at[pl.ds(0, 3)], g_send, xu)
    sent(hs.at[pl.ds(0, 3)], h_send, xu)
    sent(back_near.at[pl.ds(0, EXPERTS - FAR - 1)], b_send, xu)
    sent(cz.at[pl.ds(0, 3)], z_send, xu)


def shards(tokens, routes, route_gates, gate_weight, up_weight, down_weight):
    token_count, width = tokens.shape
    depth, block = gate_weight.shape[1:]
    dma, vmem = pltpu.SemaphoreType.DMA, pltpu.VMEM
    halves = (RING, RING, width, block)
    return pl.pallas_call(
        layer,
        out_shape=jax.ShapeDtypeStruct((token_count, width), BF16),
        in_specs=[pl.BlockSpec(memory_space=pltpu.HBM)] * 6,
        out_specs=pl.BlockSpec(memory_space=vmem),
        scratch_shapes=[
            vmem((RING, token_count, width), BF16),
            vmem((2, token_count), jnp.int32),
            vmem((2, token_count), F32),
            vmem((FAR, CAP, width), BF16),
            vmem((EXPERTS - FAR, RING, CAP, width), BF16),
            vmem((CHUNKS, PER, RING, CAP, width), BF16),
            vmem((2,) + halves, BF16),
            vmem((2,) + halves[1:], BF16),
            vmem((RING, RING * block, width), BF16),
            vmem((2, 2, block, width), BF16),
            vmem((RING, CHUNKS, ROWS, 2 * block), BF16),
            vmem((CHUNKS, ROWS, 2 * block), F32),
            vmem((RING - 1, CHUNKS, ROWS, 2 * block), BF16),
            vmem((RING, CHUNKS, ROWS, block), BF16),
            vmem((CHUNKS, PER, RING, CAP, width), BF16),
            vmem((RING - 1, FAR_CHUNKS, PER, CAP, width), BF16),
            vmem((FAR_CHUNKS, PER, CAP, width), BF16),
            vmem((FAR, CAP, width), BF16),
            vmem((EXPERTS - FAR, RING, CAP, width), BF16),
            vmem((2 * token_count, EXPERTS * CAP), BF16),
            vmem((RING, token_count, width), BF16),
            vmem((RING - 1, token_count, width), BF16),
            dma((5 + RING,)),
            dma,
            dma((RING,)),
            dma,
            dma((8,)),
            dma,
            dma((6,)),
            dma,
            dma,
            dma((EXPERTS,)),
            dma,
            dma((RING - 1, FAR_CHUNKS)),
            dma,
            dma((RING - 1, CHUNKS)),
            dma,
            dma((RING - 1, CHUNKS)),
            dma,
            dma((RING - 1, FAR_CHUNKS)),
            dma,
            dma,
            dma((EXPERTS,)),
            dma,
            dma((RING - 1,)),
        ],
        compiler_params=pltpu.CompilerParams(
            collective_id=0, has_side_effects=True, vmem_limit_bytes=62 * 1024 * 1024
        ),
    )(
        tokens,
        routes.T,
        route_gates.T,
        gate_weight.reshape(halves),
        up_weight.reshape(halves),
        down_weight[0],
    )


def solution(mesh):
    return jax.shard_map(
        shards,
        mesh=mesh,
        in_specs=(
            P("expert", "tensor"),
            P("expert", None),
            P("expert", None),
            P("expert", None, "tensor"),
            P("expert", None, "tensor"),
            P("expert", "tensor", None),
        ),
        out_specs=P("expert", "tensor"),
        check_vma=False,
    )
```

```python
import jax
import jax.numpy as jnp
from jax import lax
from jax.experimental import pallas as pl
from jax.experimental.pallas import tpu as pltpu
from jax.sharding import PartitionSpec as P

MESH = pl.DeviceIdType.MESH
F32, BF16 = jnp.float32, jnp.bfloat16
RING = 4
EXPERTS, CAP, CHUNKS = 32, 16, 4
PER = EXPERTS // CHUNKS
ROWS = PER * CAP
HOME = EXPERTS - 4
FAR_CHUNKS = 1
FAR = FAR_CHUNKS * PER


def remote(src, dst, send, recv, device):
    return pltpu.make_async_remote_copy(
        src_ref=src, dst_ref=dst, send_sem=send, recv_sem=recv, device_id=device, device_id_type=MESH
    )


def arrived(ref, sem, device):
    remote(ref, ref, sem, sem, device).wait_recv()


def sent(ref, sem, device):
    remote(ref, ref, sem, sem, device).wait_send()


def layer(
    tok_hbm, routes_hbm, gates_hbm, gate_hbm, up_hbm, down_hbm, out,
    tz, routes, gates, out_far, out_near, xs, w_in, w_out,
    gu_out, gu_own, gu_in, hs, ps, zs, sums, back, share,
    l_sem, t_send, t_recv, wi_send, wi_recv, wo_send, wo_recv, f_send, a_send, a_recv, q_send, q_recv,
    g_send, g_recv, h_send, h_recv, r_send, r_recv, s_send, s_recv,
):
    e, t = lax.axis_index("expert"), lax.axis_index("tensor")
    core, y, zl = e % 2, (e // 2) % 8, e // 16
    x, zh = t % RING, t // RING
    tokens, width = out.shape
    block = w_in.shape[-1]

    def over_x(k):
        return (e, zh * RING + (x + k) % RING)

    def over_z(k):
        return (e, ((zh + k) % RING) * RING + x)

    xu = over_x(1)

    layers, cores = (zl * 16, 16 - zl * 16), (core, 1 - core)

    def group(c, sign):
        found = []
        for dy in (4 - c, c - 3):
            rows = [((y + turn * sign * dy + 8) % 8) * 2 for turn in (1, -1)]
            found += [layers[f // 2] + rows[f % 2] + cores[f % 2] for f in range(4)]
        return found

    lists = [group(c, -1) for c in range(CHUNKS)]
    barrier = pltpu.get_barrier_semaphore()
    for k in (1, 2, 3):
        pl.semaphore_signal(barrier, inc=1, device_id=over_z(k), device_id_type=MESH)
        pl.semaphore_signal(barrier, inc=1, device_id=over_x(k), device_id_type=MESH)
    for j in range(EXPERTS):
        if j != HOME:
            pl.semaphore_signal(barrier, inc=1, device_id=(lists[j // PER][j % PER], t), device_id_type=MESH)

    smalls = [
        pltpu.make_async_copy(tok_hbm, tz.at[zh], l_sem.at[0]),
        pltpu.make_async_copy(routes_hbm, routes, l_sem.at[1]),
        pltpu.make_async_copy(gates_hbm, gates, l_sem.at[2]),
    ]
    wide = RING * width

    def columns(n):
        return pl.ds(pl.multiple_of(n * wide, wide), wide)

    loads = [
        pltpu.make_async_copy(gate_hbm.at[:, x], w_in.at[0, x], l_sem.at[3]),
        pltpu.make_async_copy(up_hbm.at[:, x], w_in.at[1, x], l_sem.at[4]),
        pltpu.make_async_copy(down_hbm.at[:, columns(zh)], w_out.at[zh], l_sem.at[5]),
    ]
    for load in smalls:
        load.start()
    for load in smalls:
        load.wait()
    pl.semaphore_wait(barrier, EXPERTS - 1 + 6)

    for k in (2, 1, 3):
        remote(tz.at[zh], tz.at[zh], t_send, t_recv.at[k], over_z(k)).start()
    for k in (2, 1, 3):
        n = (x + k) % RING
        remote(gate_hbm.at[:, n], w_in.at[0, x], wi_send, wi_recv.at[0, k - 1], over_x(k)).start()
        remote(up_hbm.at[:, n], w_in.at[1, x], wi_send, wi_recv.at[1, k - 1], over_x(k)).start()

    first, second = routes[0:1, :], routes[1:2, :]
    names = lax.broadcasted_iota(jnp.int32, (EXPERTS, tokens), 0)
    one, two = names == first, names == second
    count = (jnp.where(one, 1.0, 0.0) + jnp.where(two, 1.0, 0.0)).astype(BF16)
    earlier = lax.broadcasted_iota(jnp.int32, (tokens, tokens), 0) < lax.broadcasted_iota(
        jnp.int32, (tokens, tokens), 1
    )
    before = jnp.dot(count, jnp.where(earlier, 1.0, 0.0).astype(BF16), preferred_element_type=F32)

    def listed(route):
        f = (((route >> 4) + zl) & 1) * 2 + ((route + core) & 1)
        turn = 1 - 2 * ((route + core) & 1)
        m = ((y - ((route >> 1) & 7)) * turn) & 7
        k = jnp.where(m <= 4, jnp.maximum(2 * m - 1, 0), 16 - 2 * m)
        return ((7 - k) * 4 + f).astype(F32)

    place_one = listed(first) * CAP + jnp.sum(jnp.where(one, before, 0.0), axis=0, keepdims=True)
    place_two = listed(second) * CAP + jnp.sum(jnp.where(two, before, 0.0), axis=0, keepdims=True)
    places = lax.broadcasted_iota(jnp.int32, (EXPERTS * CAP, tokens), 0).astype(F32)
    at_one, at_two = places == place_one, places == place_two
    picks = (jnp.where(at_one, 1.0, 0.0) + jnp.where(at_two, 1.0, 0.0)).astype(BF16)

    picked = jnp.dot(picks[: FAR * CAP], tz[zh], preferred_element_type=F32).astype(BF16)
    out_far[...] = picked.reshape(FAR, CAP, width)

    for j in range(FAR):
        c, i = j // PER, j % PER
        remote(out_far.at[j], xs.at[c, i, zh], f_send, a_recv.at[c], (lists[c][i], t)).start()
    for k in (0, 1, 3, 2):
        n = (zh + 4 - k) % RING
        if k:
            arrived(tz.at[n], t_recv.at[k], xu)
        picked = jnp.dot(picks[FAR * CAP :], tz[n], preferred_element_type=F32).astype(BF16)
        out_near[:, n] = picked.reshape(EXPERTS - FAR, CAP, width)

    for j in range(FAR, EXPERTS):
        c, i = j // PER, j % PER
        if j != HOME:
            remote(out_near.at[j - FAR], xs.at[c, i], a_send, a_recv.at[c], (lists[c][i], t)).start()
    xs[HOME // PER, HOME % PER] = out_near[HOME - FAR]
    for k in (2, 1, 3):
        n = (zh + k) % RING
        remote(down_hbm.at[:, columns(n)], w_out.at[zh], wo_send, wo_recv.at[k - 1], over_z(k)).start()
    for load in loads:
        load.start()

    def spread(c, carry):
        arrived(xs.at[c, :, zh], a_recv.at[c], xu)
        for k in (2, 1, 3):
            own = xs.at[c, :, zh]
            remote(own, own, q_send, q_recv.at[k - 1, c], over_z(k)).start()
        return carry

    lax.fori_loop(0, FAR_CHUNKS, spread, 0)

    shared = jnp.where(at_one, gates[0:1, :], 0.0) + jnp.where(at_two, gates[1:2, :], 0.0)
    shared = shared.T
    coarse = shared.astype(BF16)
    share[0:tokens, :] = coarse
    share[tokens : 2 * tokens, :] = (shared - coarse.astype(F32)).astype(BF16)

    for load in loads:
        load.wait()
    for k in (1, 3, 2):
        for m in (0, 1):
            arrived(w_in.at[m, (x + 4 - k) % RING], wi_recv.at[m, k - 1], xu)

    def project(c):
        @pl.when(c < FAR_CHUNKS)
        def _():
            for k in (1, 3, 2):
                arrived(xs.at[c, :, (zh + 4 - k) % RING], q_recv.at[k - 1, c], xu)

        @pl.when((c >= FAR_CHUNKS) & (c < CHUNKS - 1))
        def _():
            arrived(xs.at[c], a_recv.at[c], xu)

        @pl.when(c == CHUNKS - 1)
        def _():
            arrived(xs.at[c, pl.ds(0, PER - 1)], a_recv.at[c], xu)

        for k in (2, 1, 3, 0):
            n = (x + k) % RING
            total = jnp.zeros((ROWS, 2 * block), F32)
            for b in range(RING):
                weights = jnp.concatenate([w_in[0, n, b], w_in[1, n, b]], axis=1)
                total += jnp.dot(xs[c, :, b].reshape(ROWS, width), weights, preferred_element_type=F32)
            if k:
                gu_out[n, c] = total.astype(BF16)
                remote(gu_out.at[n, c], gu_in.at[k - 1, c], g_send, g_recv.at[k - 1, c], over_x(k)).start()
            else:
                gu_own[c] = total

    def activate(c):
        total = gu_own[c]
        for k in (1, 3, 2):
            arrived(gu_in.at[k - 1, c], g_recv.at[k - 1, c], xu)
            total += gu_in[k - 1, c].astype(F32)
        gate, up = total[:, :block], total[:, block:]
        hs[zh, c] = (gate / (1.0 + jnp.exp(-gate)) * up).astype(BF16)
        for k in (2, 1, 3):
            remote(hs.at[zh, c], hs.at[zh, c], h_send, h_recv.at[k - 1, c], over_z(k)).start()

    def have_out():
        for k in (1, 3, 2):
            arrived(w_out.at[(zh + 4 - k) % RING], wo_recv.at[k - 1], xu)

    def expand(c):
        for k in (1, 3, 2):
            arrived(hs.at[(zh + 4 - k) % RING, c], h_recv.at[k - 1, c], xu)
        hidden = jnp.concatenate([hs[n, c] for n in range(RING)], axis=1)
        weights = w_out[...].reshape(RING * block, wide)
        for n in range(RING):
            part = jnp.dot(hidden, weights[:, n * width : (n + 1) * width], preferred_element_type=F32)
            ps[c, n] = part.astype(BF16)
        for k in (2, 1, 3):
            remote(
                ps.at[c, (x + k) % RING], zs.at[k - 1, c], r_send, r_recv.at[k - 1, c], over_x(k)
            ).start()

    def settle(c):
        total = ps[c, x].astype(F32)
        for k in (1, 3, 2):
            arrived(zs.at[k - 1, c], r_recv.at[k - 1, c], xu)
            total += zs[k - 1, c].astype(F32)
        sums[c] = total.astype(BF16).reshape(PER, CAP, width)
        sources = group(c, 1)
        for i in range(PER):

            def send(i=i):
                remote(sums.at[c, i], back.at[c * PER + i], s_send, s_recv, (sources[i], t)).start()

            pl.when(c < CHUNKS - 1)(send) if i == HOME % PER else send()

    def each(c, carry):
        project(c)
        return carry

    lax.fori_loop(0, CHUNKS, each, 0)

    def tick(s, carry):
        pl.when(s < CHUNKS)(lambda: activate(s))
        pl.when(s == 2)(have_out)
        pl.when((s >= 2) & (s < CHUNKS + 2))(lambda: expand(s - 2))
        pl.when(s >= 3)(lambda: settle(s - 3))
        return carry

    lax.fori_loop(0, CHUNKS + 3, tick, 0)
    back[HOME] = sums[HOME // PER, HOME % PER]
    arrived(back.at[pl.ds(0, EXPERTS - 1)], s_recv, xu)
    both = jnp.dot(share[...], back[...].reshape(EXPERTS * CAP, width), preferred_element_type=F32)
    out[...] = (both[:tokens] + both[tokens:]).astype(BF16)

    sent(tz.at[pl.ds(0, 3)], t_send, xu)
    sent(w_in.at[:, pl.ds(0, 3)], wi_send, xu)
    sent(w_out.at[pl.ds(0, 3)], wo_send, xu)
    sent(out_far, f_send, xu)
    sent(out_near.at[pl.ds(0, EXPERTS - FAR - 1)], a_send, xu)
    sent(xs.at[pl.ds(0, FAR_CHUNKS), :, pl.ds(0, 3)], q_send, xu)
    sent(gu_out.at[pl.ds(0, 3)], g_send, xu)
    sent(hs.at[pl.ds(0, 3)], h_send, xu)
    sent(ps.at[:, pl.ds(0, 3)], r_send, xu)
    sent(back.at[pl.ds(0, EXPERTS - 1)], s_send, xu)


def shards(tokens, routes, route_gates, gate_weight, up_weight, down_weight):
    token_count, width = tokens.shape
    depth, block = gate_weight.shape[1:]
    dma, vmem = pltpu.SemaphoreType.DMA, pltpu.VMEM
    halves = (RING, RING, width, block)
    return pl.pallas_call(
        layer,
        out_shape=jax.ShapeDtypeStruct((token_count, width), BF16),
        in_specs=[pl.BlockSpec(memory_space=pltpu.HBM)] * 6,
        out_specs=pl.BlockSpec(memory_space=vmem),
        scratch_shapes=[
            vmem((RING, token_count, width), BF16),
            vmem((2, token_count), jnp.int32),
            vmem((2, token_count), F32),
            vmem((FAR, CAP, width), BF16),
            vmem((EXPERTS - FAR, RING, CAP, width), BF16),
            vmem((CHUNKS, PER, RING, CAP, width), BF16),
            vmem((2,) + halves, BF16),
            vmem((RING, block, RING * width), BF16),
            vmem((RING, CHUNKS, ROWS, 2 * block), BF16),
            vmem((CHUNKS, ROWS, 2 * block), F32),
            vmem((RING - 1, CHUNKS, ROWS, 2 * block), BF16),
            vmem((RING, CHUNKS, ROWS, block), BF16),
            vmem((CHUNKS, RING, ROWS, width), BF16),
            vmem((RING - 1, CHUNKS, ROWS, width), BF16),
            vmem((CHUNKS, PER, CAP, width), BF16),
            vmem((EXPERTS, CAP, width), BF16),
            vmem((2 * token_count, EXPERTS * CAP), BF16),
            dma((6,)),
            dma,
            dma((RING,)),
            dma,
            dma((2, RING - 1)),
            dma,
            dma((RING - 1,)),
            dma,
            dma,
            dma((CHUNKS,)),
            dma,
            dma((RING - 1, FAR_CHUNKS)),
            dma,
            dma((RING - 1, CHUNKS)),
            dma,
            dma((RING - 1, CHUNKS)),
            dma,
            dma((RING - 1, CHUNKS)),
            dma,
            dma,
        ],
        compiler_params=pltpu.CompilerParams(
            collective_id=0, has_side_effects=True, vmem_limit_bytes=62 * 1024 * 1024
        ),
    )(
        tokens,
        routes.T,
        route_gates.T,
        gate_weight.reshape(halves),
        up_weight.reshape(halves),
        down_weight[0],
    )


def solution(mesh):
    return jax.shard_map(
        shards,
        mesh=mesh,
        in_specs=(
            P("expert", "tensor"),
            P("expert", None),
            P("expert", None),
            P("expert", None, "tensor"),
            P("expert", None, "tensor"),
            P("expert", "tensor", None),
        ),
        out_specs=P("expert", "tensor"),
        check_vma=False,
    )
```

```python
import jax
import jax.numpy as jnp
from jax import lax
from jax.experimental import pallas as pl
from jax.experimental.pallas import tpu as pltpu
from jax.sharding import PartitionSpec as P

MESH = pl.DeviceIdType.MESH
F32, BF16 = jnp.float32, jnp.bfloat16
RING = 4
EXPERTS, CAP, CHUNKS = 32, 16, 4
PER = EXPERTS // CHUNKS
ROWS = PER * CAP
HOME = EXPERTS - 4
FAR = EXPERTS // 4
FAR_CHUNKS = 1


def remote(src, dst, send, recv, device):
    return pltpu.make_async_remote_copy(
        src_ref=src, dst_ref=dst, send_sem=send, recv_sem=recv, device_id=device, device_id_type=MESH
    )


def arrived(ref, sem, device):
    remote(ref, ref, sem, sem, device).wait_recv()


def sent(ref, sem, device):
    remote(ref, ref, sem, sem, device).wait_send()


def layer(
    tok_hbm, routes_hbm, gates_hbm, gate_hbm, up_hbm, down_hbm, out,
    tz, routes, gates, out_far, out_near, xs, w_in, w_in_relay, w_out, w_out_relay,
    gu_out, gu_own, gu_in, hs, ps, zs, sums, back_far, back_near, share, cz, zr,
    l_sem, t_send, t_recv, wi_send, wi_recv, wo_send, wo_recv, f_send, a_send, a_recv, q_send, q_recv,
    g_send, g_recv, h_send, h_recv, r_send, r_recv, s_send, b_send, b_recv, z_send, z_recv,
):
    e, t = lax.axis_index("expert"), lax.axis_index("tensor")
    core, y, zl = e % 2, (e // 2) % 8, e // 16
    x, zh = t % RING, t // RING
    x_up, x_dn = (x + 1) % RING, (x + 3) % RING
    xu, xd = (e, zh * RING + x_up), (e, zh * RING + x_dn)
    tokens, width = out.shape
    block = w_in.shape[-1]

    def over_x(k):
        return (e, zh * RING + (x + k) % RING)

    def over_z(k):
        return (e, ((zh + k) % RING) * RING + x)

    layers, cores = (zl * 16, 16 - zl * 16), (core, 1 - core)

    def group(c, sign):
        found = []
        for dy in (4 - c, c - 3):
            rows = [((y + turn * sign * dy + 8) % 8) * 2 for turn in (1, -1)]
            found += [layers[f // 2] + rows[f % 2] + cores[f % 2] for f in range(4)]
        return found

    lists = [group(c, -1) for c in range(CHUNKS)]
    barrier = pltpu.get_barrier_semaphore()
    for k in (1, 2, 3):
        pl.semaphore_signal(barrier, inc=1, device_id=over_z(k), device_id_type=MESH)
        pl.semaphore_signal(barrier, inc=1, device_id=over_x(k), device_id_type=MESH)
    for j in range(EXPERTS):
        if j != HOME:
            pl.semaphore_signal(barrier, inc=1, device_id=(lists[j // PER][j % PER], t), device_id_type=MESH)

    smalls = [
        pltpu.make_async_copy(tok_hbm, tz.at[zh], l_sem.at[0]),
        pltpu.make_async_copy(routes_hbm, routes, l_sem.at[1]),
        pltpu.make_async_copy(gates_hbm, gates, l_sem.at[2]),
    ]
    mine = pl.ds(pl.multiple_of(x * block, block), block)
    loads_in = [
        pltpu.make_async_copy(gate_hbm.at[:, x], w_in.at[0, x], l_sem.at[3]),
        pltpu.make_async_copy(up_hbm.at[:, x], w_in.at[1, x], l_sem.at[4]),
    ]

    def columns(b, n):
        return pl.ds(pl.multiple_of((b * RING + n) * width, width), width)

    loads_out = [
        pltpu.make_async_copy(down_hbm.at[:, columns(b, x)], w_out.at[b, mine], l_sem.at[5 + b])
        for b in range(RING)
    ]
    for load in smalls:
        load.start()
    for load in smalls:
        load.wait()
    pl.semaphore_wait(barrier, EXPERTS - 1 + 6)

    for k in (2, 1, 3):
        remote(tz.at[zh], tz.at[zh], t_send, t_recv.at[k], over_z(k)).start()
    x_far = (x + 2) % RING
    remote(gate_hbm.at[:, x_far], w_in_relay.at[0], wi_send, wi_recv.at[0], xu).start()
    remote(up_hbm.at[:, x_far], w_in_relay.at[1], wi_send, wi_recv.at[1], xd).start()
    remote(gate_hbm.at[:, x_up], w_in.at[0, x], wi_send, wi_recv.at[2], xu).start()
    remote(gate_hbm.at[:, x_dn], w_in.at[0, x], wi_send, wi_recv.at[3], xd).start()

    first, second = routes[0:1, :], routes[1:2, :]
    names = lax.broadcasted_iota(jnp.int32, (EXPERTS, tokens), 0)
    one, two = names == first, names == second
    count = (jnp.where(one, 1.0, 0.0) + jnp.where(two, 1.0, 0.0)).astype(BF16)
    earlier = lax.broadcasted_iota(jnp.int32, (tokens, tokens), 0) < lax.broadcasted_iota(
        jnp.int32, (tokens, tokens), 1
    )
    before = jnp.dot(count, jnp.where(earlier, 1.0, 0.0).astype(BF16), preferred_element_type=F32)

    def listed(route):
        f = (((route >> 4) + zl) & 1) * 2 + ((route + core) & 1)
        turn = 1 - 2 * ((route + core) & 1)
        m = ((y - ((route >> 1) & 7)) * turn) & 7
        k = jnp.where(m <= 4, jnp.maximum(2 * m - 1, 0), 16 - 2 * m)
        return ((7 - k) * 4 + f).astype(F32)

    place_one = listed(first) * CAP + jnp.sum(jnp.where(one, before, 0.0), axis=0, keepdims=True)
    place_two = listed(second) * CAP + jnp.sum(jnp.where(two, before, 0.0), axis=0, keepdims=True)
    places = lax.broadcasted_iota(jnp.int32, (EXPERTS * CAP, tokens), 0).astype(F32)
    at_one, at_two = places == place_one, places == place_two
    picks = (jnp.where(at_one, 1.0, 0.0) + jnp.where(at_two, 1.0, 0.0)).astype(BF16)

    picked = jnp.dot(picks[: FAR * CAP], tz[zh], preferred_element_type=F32).astype(BF16)
    out_far[...] = picked.reshape(FAR, CAP, width)

    for j in range(FAR):
        c, i = j // PER, j % PER
        remote(out_far.at[j], xs.at[c, i, zh], f_send, a_recv.at[c], (lists[c][i], t)).start()
    for k in (0, 1, 3, 2):
        n = (zh + 4 - k) % RING
        if k:
            arrived(tz.at[n], t_recv.at[k], xu)
        picked = jnp.dot(picks[FAR * CAP :], tz[n], preferred_element_type=F32).astype(BF16)
        out_near[:, n] = picked.reshape(EXPERTS - FAR, CAP, width)

    for j in range(FAR, EXPERTS):
        c, i = j // PER, j % PER
        if j != HOME:
            remote(out_near.at[j - FAR], xs.at[c, i], a_send, a_recv.at[c], (lists[c][i], t)).start()
    xs[HOME // PER, HOME % PER] = out_near[HOME - FAR]
    for load in loads_in + loads_out:
        load.start()

    def spread(c, carry):
        arrived(xs.at[c, :, zh], a_recv.at[c], xu)
        for k in (2, 1, 3):
            own = xs.at[c, :, zh]
            remote(own, own, q_send, q_recv.at[k - 1, c], over_z(k)).start()
        return carry

    lax.fori_loop(0, FAR_CHUNKS, spread, 0)

    arrived(w_in_relay.at[0], wi_recv.at[0], xu)
    remote(w_in_relay.at[0], w_in.at[0, x_dn], wi_send, wi_recv.at[6], xu).start()
    arrived(w_in_relay.at[1], wi_recv.at[1], xu)
    remote(w_in_relay.at[1], w_in.at[1, x_up], wi_send, wi_recv.at[7], xd).start()
    remote(up_hbm.at[:, x_up], w_in.at[1, x], wi_send, wi_recv.at[4], xu).start()
    remote(up_hbm.at[:, x_dn], w_in.at[1, x], wi_send, wi_recv.at[5], xd).start()
    for b in (0, 1):
        remote(down_hbm.at[:, columns(b, x_far)], w_out_relay.at[0, b], wo_send, wo_recv.at[0], xu).start()
        remote(
            down_hbm.at[:, columns(b + 2, x_far)], w_out_relay.at[1, b], wo_send, wo_recv.at[1], xd
        ).start()
    for b in range(RING):
        remote(down_hbm.at[:, columns(b, x_up)], w_out.at[b, mine], wo_send, wo_recv.at[2], xu).start()
        remote(down_hbm.at[:, columns(b, x_dn)], w_out.at[b, mine], wo_send, wo_recv.at[3], xd).start()

    shared = jnp.where(at_one, gates[0:1, :], 0.0) + jnp.where(at_two, gates[1:2, :], 0.0)
    shared = shared.T
    coarse = shared.astype(BF16)
    share[0:tokens, :] = coarse
    share[tokens : 2 * tokens, :] = (shared - coarse.astype(F32)).astype(BF16)

    from_dn = pl.ds(pl.multiple_of(x_dn * block, block), block)
    from_up = pl.ds(pl.multiple_of(x_up * block, block), block)
    from_far = pl.ds(pl.multiple_of(x_far * block, block), block)

    for load in loads_in:
        load.wait()
    arrived(w_in.at[0, x_dn], wi_recv.at[2], xu)
    arrived(w_in.at[0, x_up], wi_recv.at[3], xu)
    arrived(w_in.at[1, x_dn], wi_recv.at[4], xu)
    arrived(w_in.at[1, x_up], wi_recv.at[5], xu)
    arrived(w_in.at[0, x_far], wi_recv.at[6], xu)
    arrived(w_in.at[1, x_far], wi_recv.at[7], xu)

    def project(c):
        @pl.when(c < FAR_CHUNKS)
        def _():
            for k in (1, 3, 2):
                arrived(xs.at[c, :, (zh + 4 - k) % RING], q_recv.at[k - 1, c], xu)

        @pl.when((c >= FAR_CHUNKS) & (c < CHUNKS - 1))
        def _():
            arrived(xs.at[c], a_recv.at[c], xu)

        @pl.when(c == CHUNKS - 1)
        def _():
            arrived(xs.at[c, pl.ds(0, PER - 1)], a_recv.at[c], xu)

        for k in (2, 1, 3, 0):
            n = (x + k) % RING
            total = jnp.zeros((ROWS, 2 * block), F32)
            for b in range(RING):
                weights = jnp.concatenate([w_in[0, n, b], w_in[1, n, b]], axis=1)
                total += jnp.dot(xs[c, :, b].reshape(ROWS, width), weights, preferred_element_type=F32)
            if k:
                gu_out[n, c] = total.astype(BF16)
                remote(gu_out.at[n, c], gu_in.at[k - 1, c], g_send, g_recv.at[k - 1, c], over_x(k)).start()
            else:
                gu_own[c] = total

    def activate(c):
        total = gu_own[c]
        for k in (1, 3, 2):
            arrived(gu_in.at[k - 1, c], g_recv.at[k - 1, c], xu)
            total += gu_in[k - 1, c].astype(F32)
        gate, up = total[:, :block], total[:, block:]
        hs[x, c] = (gate / (1.0 + jnp.exp(-gate)) * up).astype(BF16)
        for k in (2, 1, 3):
            remote(hs.at[x, c], hs.at[x, c], h_send, h_recv.at[k - 1, c], over_x(k)).start()

    def hand_on():
        arrived(w_out_relay.at[0], wo_recv.at[0], xu)
        low, high = pl.ds(0, 2), pl.ds(2, 2)
        remote(w_out_relay.at[0], w_out.at[low, from_dn], wo_send, wo_recv.at[4], xu).start()
        arrived(w_out_relay.at[1], wo_recv.at[1], xu)
        remote(w_out_relay.at[1], w_out.at[high, from_up], wo_send, wo_recv.at[5], xd).start()

    def have_out():
        for load in loads_out:
            load.wait()
        low, high = pl.ds(0, 2), pl.ds(2, 2)
        arrived(w_out.at[:, from_dn], wo_recv.at[2], xu)
        arrived(w_out.at[:, from_up], wo_recv.at[3], xu)
        arrived(w_out.at[low, from_far], wo_recv.at[4], xu)
        arrived(w_out.at[high, from_far], wo_recv.at[5], xu)

    def expand(c):
        for k in (1, 3, 2):
            n = (x + 4 - k) % RING
            arrived(hs.at[n, c], h_recv.at[k - 1, c], xu)
        hidden = jnp.concatenate([hs[n, c] for n in range(RING)], axis=1)
        for b in range(RING):
            part = jnp.dot(hidden, w_out[b], preferred_element_type=F32).astype(BF16)
            ps[c, :, b] = part.reshape(PER, CAP, width)

        @pl.when(c < FAR_CHUNKS)
        def _():
            for k in (2, 1, 3):
                remote(
                    ps.at[c, :, (zh + k) % RING], zs.at[k - 1, c], r_send, r_recv.at[k - 1, c], over_z(k)
                ).start()

        @pl.when(c >= FAR_CHUNKS)
        def _():
            sources = group(c, 1)
            for i in range(PER):

                def send(i=i):
                    remote(
                        ps.at[c, i], back_near.at[(c - FAR_CHUNKS) * PER + i], b_send, b_recv.at[1],
                        (sources[i], t),
                    ).start()

                pl.when(c < CHUNKS - 1)(send) if i == HOME % PER else send()

    def settle(c):
        total = ps[c, :, zh].astype(F32)
        for k in (1, 3, 2):
            arrived(zs.at[k - 1, c], r_recv.at[k - 1, c], xu)
            total += zs[k - 1, c].astype(F32)
        sums[c] = total.astype(BF16)

        sources = group(c, 1)
        for i in range(PER):
            remote(
                sums.at[c, i], back_far.at[c * PER + i], s_send, b_recv.at[0], (sources[i], t)
            ).start()

    def tick(s, carry):
        @pl.when(s < CHUNKS)
        def _():
            project(s)

        pl.when(s == 1)(hand_on)

        @pl.when((s >= 1) & (s <= CHUNKS))
        def _():
            activate(s - 1)

        pl.when(s == 2)(have_out)

        @pl.when(s >= 2)
        def _():
            expand(s - 2)

        @pl.when((s >= 3) & (s < 3 + FAR_CHUNKS))
        def _():
            settle(s - 3)

        return carry

    lax.fori_loop(0, CHUNKS + 2, tick, 0)
    back_near[HOME - FAR] = ps[HOME // PER, HOME % PER]

    def weigh(shares, returned):
        both = jnp.dot(shares, returned.reshape(returned.shape[0] * CAP, width), preferred_element_type=F32)
        return both[:tokens] + both[tokens:]

    def combine(n):
        return weigh(share[:, FAR * CAP :], back_near[:, n])

    arrived(back_far, b_recv.at[0], xu)
    total = weigh(share[:, : FAR * CAP], back_far[...])
    arrived(back_near.at[pl.ds(0, EXPERTS - FAR - 1)], b_recv.at[1], xu)
    for k in (2, 1, 3):
        n = (zh + k) % RING
        cz[n] = combine(n).astype(BF16)
        remote(cz.at[n], zr.at[k - 1], z_send, z_recv.at[k - 1], over_z(k)).start()
    total += combine(zh)
    for k in (1, 3, 2):
        arrived(zr.at[k - 1], z_recv.at[k - 1], xu)
        total += zr[k - 1].astype(F32)
    out[...] = total.astype(BF16)

    sent(tz.at[pl.ds(0, 3)], t_send, xu)
    sent(w_in, wi_send, xu)
    sent(w_out, wo_send, xu)
    sent(out_far, f_send, xu)
    sent(out_near.at[pl.ds(0, EXPERTS - FAR - 1)], a_send, xu)
    some = (pl.ds(0, FAR_CHUNKS), slice(None), pl.ds(0, 3))
    sent(xs.at[some], q_send, xu)
    sent(ps.at[some], r_send, xu)
    sent(back_far, s_send, xu)
    sent(gu_out.at[pl.ds(0, 3)], g_send, xu)
    sent(hs.at[pl.ds(0, 3)], h_send, xu)
    sent(back_near.at[pl.ds(0, EXPERTS - FAR - 1)], b_send, xu)
    sent(cz.at[pl.ds(0, 3)], z_send, xu)


def shards(tokens, routes, route_gates, gate_weight, up_weight, down_weight):
    token_count, width = tokens.shape
    depth, block = gate_weight.shape[1:]
    dma, vmem = pltpu.SemaphoreType.DMA, pltpu.VMEM
    halves = (RING, RING, width, block)
    return pl.pallas_call(
        layer,
        out_shape=jax.ShapeDtypeStruct((token_count, width), BF16),
        in_specs=[pl.BlockSpec(memory_space=pltpu.HBM)] * 6,
        out_specs=pl.BlockSpec(memory_space=vmem),
        scratch_shapes=[
            vmem((RING, token_count, width), BF16),
            vmem((2, token_count), jnp.int32),
            vmem((2, token_count), F32),
            vmem((FAR, CAP, width), BF16),
            vmem((EXPERTS - FAR, RING, CAP, width), BF16),
            vmem((CHUNKS, PER, RING, CAP, width), BF16),
            vmem((2,) + halves, BF16),
            vmem((2,) + halves[1:], BF16),
            vmem((RING, RING * block, width), BF16),
            vmem((2, 2, block, width), BF16),
            vmem((RING, CHUNKS, ROWS, 2 * block), BF16),
            vmem((CHUNKS, ROWS, 2 * block), F32),
            vmem((RING - 1, CHUNKS, ROWS, 2 * block), BF16),
            vmem((RING, CHUNKS, ROWS, block), BF16),
            vmem((CHUNKS, PER, RING, CAP, width), BF16),
            vmem((RING - 1, FAR_CHUNKS, PER, CAP, width), BF16),
            vmem((FAR_CHUNKS, PER, CAP, width), BF16),
            vmem((FAR, CAP, width), BF16),
            vmem((EXPERTS - FAR, RING, CAP, width), BF16),
            vmem((2 * token_count, EXPERTS * CAP), BF16),
            vmem((RING, token_count, width), BF16),
            vmem((RING - 1, token_count, width), BF16),
            dma((5 + RING,)),
            dma,
            dma((RING,)),
            dma,
            dma((8,)),
            dma,
            dma((6,)),
            dma,
            dma,
            dma((CHUNKS,)),
            dma,
            dma((RING - 1, FAR_CHUNKS)),
            dma,
            dma((RING - 1, CHUNKS)),
            dma,
            dma((RING - 1, CHUNKS)),
            dma,
            dma((RING - 1, FAR_CHUNKS)),
            dma,
            dma,
            dma((2,)),
            dma,
            dma((RING - 1,)),
        ],
        compiler_params=pltpu.CompilerParams(
            collective_id=0, has_side_effects=True, vmem_limit_bytes=62 * 1024 * 1024
        ),
    )(
        tokens,
        routes.T,
        route_gates.T,
        gate_weight.reshape(halves),
        up_weight.reshape(halves),
        down_weight[0],
    )


def solution(mesh):
    return jax.shard_map(
        shards,
        mesh=mesh,
        in_specs=(
            P("expert", "tensor"),
            P("expert", None),
            P("expert", None),
            P("expert", None, "tensor"),
            P("expert", None, "tensor"),
            P("expert", "tensor", None),
        ),
        out_specs=P("expert", "tensor"),
        check_vma=False,
    )
```

```python
import jax
import jax.numpy as jnp
from jax import lax
from jax.experimental import pallas as pl
from jax.experimental.pallas import tpu as pltpu
from jax.sharding import PartitionSpec as P

MESH = pl.DeviceIdType.MESH
F32, BF16 = jnp.float32, jnp.bfloat16
RING = 4
EXPERTS, CAP, CHUNKS = 32, 16, 4
PER = EXPERTS // CHUNKS
ROWS = PER * CAP
HOME = EXPERTS - 4
FAR = EXPERTS // 4
FAR_CHUNKS = 1


def remote(src, dst, send, recv, device):
    return pltpu.make_async_remote_copy(
        src_ref=src, dst_ref=dst, send_sem=send, recv_sem=recv, device_id=device, device_id_type=MESH
    )


def arrived(ref, sem, device):
    remote(ref, ref, sem, sem, device).wait_recv()


def sent(ref, sem, device):
    remote(ref, ref, sem, sem, device).wait_send()


def layer(
    tok_hbm, routes_hbm, gates_hbm, gate_hbm, up_hbm, down_hbm, out,
    tz, routes, gates, out_far, out_near, xs, w_in, w_in_relay, w_out, w_out_relay,
    gu_out, gu_own, gu_in, hs, ps, zs, sums, back_far, back_near, share, cz, zr,
    l_sem, t_send, t_recv, wi_send, wi_recv, wo_send, wo_recv, f_send, a_send, a_recv, q_send, q_recv,
    g_send, g_recv, h_send, h_recv, r_send, r_recv, s_send, b_send, b_recv, z_send, z_recv,
):
    e, t = lax.axis_index("expert"), lax.axis_index("tensor")
    core, y, zl = e % 2, (e // 2) % 8, e // 16
    x, zh = t % RING, t // RING
    x_up, x_dn = (x + 1) % RING, (x + 3) % RING
    xu, xd = (e, zh * RING + x_up), (e, zh * RING + x_dn)
    tokens, width = out.shape
    block = w_in.shape[-1]

    def over_x(k):
        return (e, zh * RING + (x + k) % RING)

    def over_z(k):
        return (e, ((zh + k) % RING) * RING + x)

    layers, cores = (zl * 16, 16 - zl * 16), (core, 1 - core)

    def group(c, sign):
        found = []
        for dy in (4 - c, c - 3):
            rows = [((y + turn * sign * dy + 8) % 8) * 2 for turn in (1, -1)]
            found += [layers[f // 2] + rows[f % 2] + cores[f % 2] for f in range(4)]
        return found

    lists = [group(c, -1) for c in range(CHUNKS)]
    smalls = [
        pltpu.make_async_copy(tok_hbm, tz.at[zh], l_sem.at[0]),
        pltpu.make_async_copy(routes_hbm, routes, l_sem.at[1]),
        pltpu.make_async_copy(gates_hbm, gates, l_sem.at[2]),
    ]
    for load in smalls:
        load.start()
    barrier = pltpu.get_barrier_semaphore()
    for k in (1, 2, 3):
        pl.semaphore_signal(barrier, inc=1, device_id=over_z(k), device_id_type=MESH)
        pl.semaphore_signal(barrier, inc=1, device_id=over_x(k), device_id_type=MESH)
    for j in range(EXPERTS):
        if j != HOME:
            pl.semaphore_signal(barrier, inc=1, device_id=(lists[j // PER][j % PER], t), device_id_type=MESH)

    mine = pl.ds(pl.multiple_of(x * block, block), block)
    loads_in = [
        pltpu.make_async_copy(gate_hbm.at[:, x], w_in.at[0, x], l_sem.at[3]),
        pltpu.make_async_copy(up_hbm.at[:, x], w_in.at[1, x], l_sem.at[4]),
    ]

    def columns(b, n):
        return pl.ds(pl.multiple_of((b * RING + n) * width, width), width)

    loads_out = [
        pltpu.make_async_copy(down_hbm.at[:, columns(b, x)], w_out.at[b, mine], l_sem.at[5 + b])
        for b in range(RING)
    ]
    pl.semaphore_wait(barrier, EXPERTS - 1 + 6)
    for load in smalls:
        load.wait()

    for k in (2, 1, 3):
        remote(tz.at[zh], tz.at[zh], t_send, t_recv.at[k], over_z(k)).start()
    x_far = (x + 2) % RING
    remote(gate_hbm.at[:, x_far], w_in_relay.at[0], wi_send, wi_recv.at[0], xu).start()
    remote(up_hbm.at[:, x_far], w_in_relay.at[1], wi_send, wi_recv.at[1], xd).start()
    remote(gate_hbm.at[:, x_up], w_in.at[0, x], wi_send, wi_recv.at[2], xu).start()
    remote(gate_hbm.at[:, x_dn], w_in.at[0, x], wi_send, wi_recv.at[3], xd).start()

    first, second = routes[0:1, :], routes[1:2, :]
    names = lax.broadcasted_iota(jnp.int32, (EXPERTS, tokens), 0)
    one, two = names == first, names == second
    count = (jnp.where(one, 1.0, 0.0) + jnp.where(two, 1.0, 0.0)).astype(BF16)
    earlier = lax.broadcasted_iota(jnp.int32, (tokens, tokens), 0) < lax.broadcasted_iota(
        jnp.int32, (tokens, tokens), 1
    )
    before = jnp.dot(count, jnp.where(earlier, 1.0, 0.0).astype(BF16), preferred_element_type=F32)

    def listed(route):
        f = (((route >> 4) + zl) & 1) * 2 + ((route + core) & 1)
        turn = 1 - 2 * ((route + core) & 1)
        m = ((y - ((route >> 1) & 7)) * turn) & 7
        k = jnp.where(m <= 4, jnp.maximum(2 * m - 1, 0), 16 - 2 * m)
        return ((7 - k) * 4 + f).astype(F32)

    place_one = listed(first) * CAP + jnp.sum(jnp.where(one, before, 0.0), axis=0, keepdims=True)
    place_two = listed(second) * CAP + jnp.sum(jnp.where(two, before, 0.0), axis=0, keepdims=True)
    places = lax.broadcasted_iota(jnp.int32, (EXPERTS * CAP, tokens), 0).astype(F32)
    at_one, at_two = places == place_one, places == place_two
    picks = (jnp.where(at_one, 1.0, 0.0) + jnp.where(at_two, 1.0, 0.0)).astype(BF16)

    picked = jnp.dot(picks[: FAR * CAP], tz[zh], preferred_element_type=F32).astype(BF16)
    out_far[...] = picked.reshape(FAR, CAP, width)

    for j in range(FAR):
        c, i = j // PER, j % PER
        remote(out_far.at[j], xs.at[c, i, zh], f_send, a_recv.at[c], (lists[c][i], t)).start()
    for k in (0, 1, 3, 2):
        n = (zh + 4 - k) % RING
        if k:
            arrived(tz.at[n], t_recv.at[k], xu)
        picked = jnp.dot(picks[FAR * CAP :], tz[n], preferred_element_type=F32).astype(BF16)
        out_near[:, n] = picked.reshape(EXPERTS - FAR, CAP, width)

    for j in range(FAR, EXPERTS):
        c, i = j // PER, j % PER
        if j != HOME:
            remote(out_near.at[j - FAR], xs.at[c, i], a_send, a_recv.at[c], (lists[c][i], t)).start()
    xs[HOME // PER, HOME % PER] = out_near[HOME - FAR]
    for load in loads_in + loads_out:
        load.start()

    def spread(c, carry):
        arrived(xs.at[c, :, zh], a_recv.at[c], xu)
        for k in (2, 1, 3):
            own = xs.at[c, :, zh]
            remote(own, own, q_send, q_recv.at[k - 1, c], over_z(k)).start()
        return carry

    lax.fori_loop(0, FAR_CHUNKS, spread, 0)

    arrived(w_in_relay.at[0], wi_recv.at[0], xu)
    remote(w_in_relay.at[0], w_in.at[0, x_dn], wi_send, wi_recv.at[6], xu).start()
    arrived(w_in_relay.at[1], wi_recv.at[1], xu)
    remote(w_in_relay.at[1], w_in.at[1, x_up], wi_send, wi_recv.at[7], xd).start()
    remote(up_hbm.at[:, x_up], w_in.at[1, x], wi_send, wi_recv.at[4], xu).start()
    remote(up_hbm.at[:, x_dn], w_in.at[1, x], wi_send, wi_recv.at[5], xd).start()
    for b in (0, 1):
        remote(down_hbm.at[:, columns(b, x_far)], w_out_relay.at[0, b], wo_send, wo_recv.at[0], xu).start()
        remote(
            down_hbm.at[:, columns(b + 2, x_far)], w_out_relay.at[1, b], wo_send, wo_recv.at[1], xd
        ).start()
    for b in range(RING):
        remote(down_hbm.at[:, columns(b, x_up)], w_out.at[b, mine], wo_send, wo_recv.at[2], xu).start()
        remote(down_hbm.at[:, columns(b, x_dn)], w_out.at[b, mine], wo_send, wo_recv.at[3], xd).start()

    shared = jnp.where(at_one, gates[0:1, :], 0.0) + jnp.where(at_two, gates[1:2, :], 0.0)
    shared = shared.T
    coarse = shared.astype(BF16)
    share[0:tokens, :] = coarse
    share[tokens : 2 * tokens, :] = (shared - coarse.astype(F32)).astype(BF16)

    from_dn = pl.ds(pl.multiple_of(x_dn * block, block), block)
    from_up = pl.ds(pl.multiple_of(x_up * block, block), block)
    from_far = pl.ds(pl.multiple_of(x_far * block, block), block)

    for load in loads_in:
        load.wait()
    arrived(w_in.at[0, x_dn], wi_recv.at[2], xu)
    arrived(w_in.at[0, x_up], wi_recv.at[3], xu)
    arrived(w_in.at[1, x_dn], wi_recv.at[4], xu)
    arrived(w_in.at[1, x_up], wi_recv.at[5], xu)
    arrived(w_in.at[0, x_far], wi_recv.at[6], xu)
    arrived(w_in.at[1, x_far], wi_recv.at[7], xu)

    def project(c):
        @pl.when(c < FAR_CHUNKS)
        def _():
            for k in (1, 3, 2):
                arrived(xs.at[c, :, (zh + 4 - k) % RING], q_recv.at[k - 1, c], xu)

        @pl.when((c >= FAR_CHUNKS) & (c < CHUNKS - 1))
        def _():
            arrived(xs.at[c], a_recv.at[c], xu)

        @pl.when(c == CHUNKS - 1)
        def _():
            arrived(xs.at[c, pl.ds(0, PER - 1)], a_recv.at[c], xu)

        for k in (2, 1, 3, 0):
            n = (x + k) % RING
            total = jnp.zeros((ROWS, 2 * block), F32)
            for b in range(RING):
                weights = jnp.concatenate([w_in[0, n, b], w_in[1, n, b]], axis=1)
                total += jnp.dot(xs[c, :, b].reshape(ROWS, width), weights, preferred_element_type=F32)
            if k:
                gu_out[n, c] = total.astype(BF16)
                remote(gu_out.at[n, c], gu_in.at[k - 1, c], g_send, g_recv.at[k - 1, c], over_x(k)).start()
            else:
                gu_own[c] = total

    def activate(c):
        total = gu_own[c]
        for k in (1, 3, 2):
            arrived(gu_in.at[k - 1, c], g_recv.at[k - 1, c], xu)
            total += gu_in[k - 1, c].astype(F32)
        gate, up = total[:, :block], total[:, block:]
        hs[x, c] = (gate / (1.0 + jnp.exp(-gate)) * up).astype(BF16)
        for k in (2, 1, 3):
            remote(hs.at[x, c], hs.at[x, c], h_send, h_recv.at[k - 1, c], over_x(k)).start()

    def hand_on():
        arrived(w_out_relay.at[0], wo_recv.at[0], xu)
        low, high = pl.ds(0, 2), pl.ds(2, 2)
        remote(w_out_relay.at[0], w_out.at[low, from_dn], wo_send, wo_recv.at[4], xu).start()
        arrived(w_out_relay.at[1], wo_recv.at[1], xu)
        remote(w_out_relay.at[1], w_out.at[high, from_up], wo_send, wo_recv.at[5], xd).start()

    def have_out():
        for load in loads_out:
            load.wait()
        low, high = pl.ds(0, 2), pl.ds(2, 2)
        arrived(w_out.at[:, from_dn], wo_recv.at[2], xu)
        arrived(w_out.at[:, from_up], wo_recv.at[3], xu)
        arrived(w_out.at[low, from_far], wo_recv.at[4], xu)
        arrived(w_out.at[high, from_far], wo_recv.at[5], xu)

    def expand(c):
        for k in (1, 3, 2):
            n = (x + 4 - k) % RING
            arrived(hs.at[n, c], h_recv.at[k - 1, c], xu)
        hidden = jnp.concatenate([hs[n, c] for n in range(RING)], axis=1)
        for b in range(RING):
            part = jnp.dot(hidden, w_out[b], preferred_element_type=F32).astype(BF16)
            ps[c, :, b] = part.reshape(PER, CAP, width)

        @pl.when(c < FAR_CHUNKS)
        def _():
            for k in (2, 1, 3):
                remote(
                    ps.at[c, :, (zh + k) % RING], zs.at[k - 1, c], r_send, r_recv.at[k - 1, c], over_z(k)
                ).start()

        @pl.when(c >= FAR_CHUNKS)
        def _():
            sources = group(c, 1)
            for i in range(PER):

                def send(i=i):
                    remote(
                        ps.at[c, i], back_near.at[(c - FAR_CHUNKS) * PER + i], b_send, b_recv.at[1],
                        (sources[i], t),
                    ).start()

                pl.when(c < CHUNKS - 1)(send) if i == HOME % PER else send()

    def settle(c):
        total = ps[c, :, zh].astype(F32)
        for k in (1, 3, 2):
            arrived(zs.at[k - 1, c], r_recv.at[k - 1, c], xu)
            total += zs[k - 1, c].astype(F32)
        sums[c] = total.astype(BF16)

        sources = group(c, 1)
        for i in range(PER):
            remote(
                sums.at[c, i], back_far.at[c * PER + i], s_send, b_recv.at[0], (sources[i], t)
            ).start()

    def tick(s, carry):
        @pl.when(s < CHUNKS)
        def _():
            project(s)

        pl.when(s == 1)(hand_on)

        @pl.when((s >= 1) & (s <= CHUNKS))
        def _():
            activate(s - 1)

        pl.when(s == 2)(have_out)

        @pl.when(s >= 2)
        def _():
            expand(s - 2)

        @pl.when((s >= 3) & (s < 3 + FAR_CHUNKS))
        def _():
            settle(s - 3)

        return carry

    lax.fori_loop(0, CHUNKS + 2, tick, 0)
    back_near[HOME - FAR] = ps[HOME // PER, HOME % PER]

    def weigh(shares, returned):
        both = jnp.dot(shares, returned.reshape(returned.shape[0] * CAP, width), preferred_element_type=F32)
        return both[:tokens] + both[tokens:]

    def combine(n):
        return weigh(share[:, FAR * CAP :], back_near[:, n])

    arrived(back_far, b_recv.at[0], xu)
    total = weigh(share[:, : FAR * CAP], back_far[...])
    arrived(back_near.at[pl.ds(0, EXPERTS - FAR - 1)], b_recv.at[1], xu)
    for k in (2, 1, 3):
        n = (zh + k) % RING
        cz[n] = combine(n).astype(BF16)
        remote(cz.at[n], zr.at[k - 1], z_send, z_recv.at[k - 1], over_z(k)).start()
    total += combine(zh)
    for k in (1, 3, 2):
        arrived(zr.at[k - 1], z_recv.at[k - 1], xu)
        total += zr[k - 1].astype(F32)
    out[...] = total.astype(BF16)

    sent(tz.at[pl.ds(0, 3)], t_send, xu)
    sent(w_in, wi_send, xu)
    sent(w_out, wo_send, xu)
    sent(out_far, f_send, xu)
    sent(out_near.at[pl.ds(0, EXPERTS - FAR - 1)], a_send, xu)
    some = (pl.ds(0, FAR_CHUNKS), slice(None), pl.ds(0, 3))
    sent(xs.at[some], q_send, xu)
    sent(ps.at[some], r_send, xu)
    sent(back_far, s_send, xu)
    sent(gu_out.at[pl.ds(0, 3)], g_send, xu)
    sent(hs.at[pl.ds(0, 3)], h_send, xu)
    sent(back_near.at[pl.ds(0, EXPERTS - FAR - 1)], b_send, xu)
    sent(cz.at[pl.ds(0, 3)], z_send, xu)


def shards(tokens, routes, route_gates, gate_weight, up_weight, down_weight):
    token_count, width = tokens.shape
    depth, block = gate_weight.shape[1:]
    dma, vmem = pltpu.SemaphoreType.DMA, pltpu.VMEM
    halves = (RING, RING, width, block)
    return pl.pallas_call(
        layer,
        out_shape=jax.ShapeDtypeStruct((token_count, width), BF16),
        in_specs=[pl.BlockSpec(memory_space=pltpu.HBM)] * 6,
        out_specs=pl.BlockSpec(memory_space=vmem),
        scratch_shapes=[
            vmem((RING, token_count, width), BF16),
            vmem((2, token_count), jnp.int32),
            vmem((2, token_count), F32),
            vmem((FAR, CAP, width), BF16),
            vmem((EXPERTS - FAR, RING, CAP, width), BF16),
            vmem((CHUNKS, PER, RING, CAP, width), BF16),
            vmem((2,) + halves, BF16),
            vmem((2,) + halves[1:], BF16),
            vmem((RING, RING * block, width), BF16),
            vmem((2, 2, block, width), BF16),
            vmem((RING, CHUNKS, ROWS, 2 * block), BF16),
            vmem((CHUNKS, ROWS, 2 * block), F32),
            vmem((RING - 1, CHUNKS, ROWS, 2 * block), BF16),
            vmem((RING, CHUNKS, ROWS, block), BF16),
            vmem((CHUNKS, PER, RING, CAP, width), BF16),
            vmem((RING - 1, FAR_CHUNKS, PER, CAP, width), BF16),
            vmem((FAR_CHUNKS, PER, CAP, width), BF16),
            vmem((FAR, CAP, width), BF16),
            vmem((EXPERTS - FAR, RING, CAP, width), BF16),
            vmem((2 * token_count, EXPERTS * CAP), BF16),
            vmem((RING, token_count, width), BF16),
            vmem((RING - 1, token_count, width), BF16),
            dma((5 + RING,)),
            dma,
            dma((RING,)),
            dma,
            dma((8,)),
            dma,
            dma((6,)),
            dma,
            dma,
            dma((CHUNKS,)),
            dma,
            dma((RING - 1, FAR_CHUNKS)),
            dma,
            dma((RING - 1, CHUNKS)),
            dma,
            dma((RING - 1, CHUNKS)),
            dma,
            dma((RING - 1, FAR_CHUNKS)),
            dma,
            dma,
            dma((2,)),
            dma,
            dma((RING - 1,)),
        ],
        compiler_params=pltpu.CompilerParams(
            collective_id=0, has_side_effects=True, vmem_limit_bytes=62 * 1024 * 1024
        ),
    )(
        tokens,
        routes.T,
        route_gates.T,
        gate_weight.reshape(halves),
        up_weight.reshape(halves),
        down_weight[0],
    )


def solution(mesh):
    return jax.shard_map(
        shards,
        mesh=mesh,
        in_specs=(
            P("expert", "tensor"),
            P("expert", None),
            P("expert", None),
            P("expert", None, "tensor"),
            P("expert", None, "tensor"),
            P("expert", "tensor", None),
        ),
        out_specs=P("expert", "tensor"),
        check_vma=False,
    )
```
